32 devices in a mesh: orb: 16 (over z, y, core), slab: 2 (over x).
Axes of the slice: x: 2, y: 2, z: 4, core: 2. Of those that a mesh axis runs over, the one named last changes fastest.
Arguments:
- orbitals: bfloat16 [512, 8192], P('orb', 'slab'), may hold values from -6 to 6
- eigenpotentials: bfloat16 [1024, 8192], P(None, 'slab'), may hold values from -0.0625 to 0.0625
- screening: float32 [1024], replicated, may hold values from 0.02 to 2
- trial_vectors: bfloat16 [16, 16384], P(None, 'orb'), may hold values from -0.0029296875 to 0.0029296875
- pair_index: int32 [2, 16384], P(None, 'orb'), may hold values from -1 to 511, as said below
Outputs:
- direct: float32 [16, 16384], P(None, 'orb')
The draws below stay inside these ranges and needn't reach their ends.
Inputs may be any that keep to these rules, and one draw needn't show every extreme that they name: `pair_index`: each column is a pair (i, j) of two different orbitals, or holds -1 in both rows for an empty slot. The 1024 slots of one pair owner (one device of orb) hold its pairs; in every draw some owner has all of its slots used.
All inputs are finite; a program needn't handle non-finite values.
Results may differ from the reference program's by a relative error of at most 0.0091.
Values may be sent and summed in bfloat16 or wider, within the bound.
A program may use at most 128 MiB of HBM per device.

```python
import math
import jax
import jax.numpy as jnp
from jax import lax

ORBS = 512
NEIG = 1024
NB = 16
P_DEV = 1024
NGRID = 8192
PAIRS = 16384


def draw_pair_index(key, part):
    owners = PAIRS // P_DEV
    keys = jax.random.split(jax.random.fold_in(key, 17), 6)
    counts = jax.random.randint(keys[0], (owners,), P_DEV // 4, P_DEV // 2 + 1)
    full_owner = jax.random.randint(keys[1], (), 0, owners)
    counts = jnp.where(jnp.arange(owners) == full_owner, P_DEV, counts)
    left_draw = jax.random.randint(keys[2], (PAIRS,), 0, ORBS)
    right_draw = jax.random.randint(keys[3], (PAIRS,), 0, ORBS)
    shuffle_table = jax.random.permutation(keys[4], ORBS).astype(jnp.int32)
    first_orbital = jnp.take(shuffle_table, left_draw * right_draw // ORBS)
    offsets = jax.random.randint(keys[5], (PAIRS,), 1, ORBS)
    second_orbital = (first_orbital + offsets) % ORBS
    slots = jnp.arange(PAIRS) % P_DEV
    owner_ids = jnp.arange(PAIRS) // P_DEV
    is_live = slots < jnp.take(counts, owner_ids)
    first_orbital = jnp.where(is_live, first_orbital, -1)
    second_orbital = jnp.where(is_live, second_orbital, -1)
    return jnp.stack([first_orbital, second_orbital]).astype(jnp.int32)


def block_scale(key, extent, shards, least, high):
    def one(axis_at, blocks):
        draws = jax.random.uniform(jax.random.fold_in(jax.random.fold_in(key, 6), axis_at), (blocks,), jnp.float32, least / len(shards), high / len(shards))
        return jnp.repeat(jnp.exp(draws), extent[axis_at] // blocks).reshape((-1,) + (1,) * (len(extent) - axis_at - 1))

    loudness = one(*shards[0])
    for cut in shards[1:]:
        loudness = loudness * one(*cut)
    return loudness


def gaussian(rng, dims, scale, most, shards=(), dtype=jnp.bfloat16):
    loudness = block_scale(rng, dims, shards, -0.22, 0.18) if shards else 1.0
    values = jax.random.normal(rng, dims, jnp.float32) * scale * loudness
    return jnp.minimum(jnp.maximum(values, -most), most).astype(dtype)


def setup_inputs(seed: int = 0) -> dict:
    streams_of = jax.random.split(jax.random.key(seed), 6)
    orbitals = gaussian(streams_of[0], (ORBS, NGRID), 1.0, 6.0, ((0, 16), (1, 2)))
    eigenpotentials = gaussian(streams_of[1], (NEIG, NGRID), NGRID ** -0.5, 0.0625, ((1, 2),))
    screening = jnp.clip(jnp.exp(jax.random.uniform(streams_of[2], (NEIG,), jnp.float32, math.log(0.02), math.log(2.0))), 0.02, 2.0)
    trial_vectors = gaussian(streams_of[3], (NB, PAIRS), (PAIRS * NEIG // 4) ** -0.5, 0.0029296875, ((1, 16),))
    pair_index = draw_pair_index(jax.random.fold_in(streams_of[5], 71), 0)
    return {"orbitals": orbitals, "eigenpotentials": eigenpotentials, "screening": screening, "trial_vectors": trial_vectors, "pair_index": pair_index}


def block_density(orbitals, index_block):
    is_live = index_block[0] >= 0
    first_rows = jnp.take(orbitals, jnp.maximum(index_block[0], 0).astype(jnp.int32), axis=0).astype(jnp.float32)
    second_rows = jnp.take(orbitals, jnp.maximum(index_block[1], 0).astype(jnp.int32), axis=0).astype(jnp.float32)
    product = jnp.where(is_live[:, None], first_rows * second_rows, jnp.zeros((), jnp.float32))
    return product.astype(jnp.bfloat16)


def reference(orbitals, eigenpotentials, screening, trial_vectors, pair_index):
    blocks = PAIRS // P_DEV
    index_blocks = pair_index.reshape(2, blocks, P_DEV).transpose(1, 0, 2)
    trial_blocks = trial_vectors.reshape(NB, blocks, P_DEV).transpose(1, 0, 2)
    potentials = eigenpotentials.astype(jnp.float32)

    def accumulate(carry, item):
        index_block, trial_block = item
        density = block_density(orbitals, index_block).astype(jnp.float32)
        term = jnp.dot(trial_block.astype(jnp.float32), density, precision=lax.Precision.HIGHEST)
        return carry + term, None

    field_sum, unused = lax.scan(accumulate, jnp.zeros((NB, NGRID), jnp.float32), (index_blocks, trial_blocks))
    projected = lax.dot_general(field_sum, potentials, (((1,), (1,)), ((), ())), precision=lax.Precision.HIGHEST)
    screened = projected * screening.astype(jnp.float32)[None, :]
    potential = jnp.dot(screened, potentials, precision=lax.Precision.HIGHEST)

    def apply_block(index_block):
        density = block_density(orbitals, index_block).astype(jnp.float32)
        return lax.dot_general(potential, density, (((1,), (1,)), ((), ())), precision=lax.Precision.HIGHEST)

    direct_blocks = lax.map(apply_block, index_blocks)
    return direct_blocks.transpose(1, 0, 2).reshape(NB, PAIRS)
```

```python
import functools

import jax
import jax.numpy as jnp
from jax import lax
from jax.experimental import pallas as pl
from jax.experimental.pallas import tpu as pltpu
from jax.sharding import PartitionSpec as P

QUAD = 4
LANES = 128
MESH_ID = pl.DeviceIdType.MESH
VMEM_SPEC = pl.BlockSpec(memory_space=pltpu.VMEM)
ANY_SPEC = pl.BlockSpec(memory_space=pl.ANY)


def greet(peers):
    barrier = pltpu.get_barrier_semaphore()
    for peer in peers:
        pl.semaphore_signal(barrier, inc=1, device_id=peer, device_id_type=MESH_ID)
    return lambda: pl.semaphore_wait(barrier, len(peers))


def columns(start, size):
    return pl.ds(pl.multiple_of(start * size, size), size)


def spread_kernel(
    groups, orb_ref, trial_ref, pair_ref, table_ref, trials_ref, pairs_ref,
    own_sem, a_send, a_recv, y_send, y_recv, c_send, c_recv, t_send, t_recv, p_send, p_recv,
):
    me = lax.axis_index("orb")
    group, place = me // QUAD, lax.rem(me, QUAD)
    core = place + 1 - 2 * lax.rem(place, 2)
    side = lax.rem(place + 2, QUAD)
    width = table_ref.shape[2]

    def device(g, q):
        return {"orb": g * QUAD + q}

    others = [lax.rem(group + k, groups) for k in range(1, groups)]
    sources = [lax.rem(group + groups - k, groups) for k in range(1, groups)]
    ready = greet(
        [device(g, place) for g in others] + [device(group, core), device(group, side)]
    )

    def out_block(g):
        return orb_ref.at[:, columns(g, width)]

    own = pltpu.make_async_copy(out_block(group), table_ref.at[me], own_sem.at[0])
    own_t = pltpu.make_async_copy(trial_ref, trials_ref.at[group], own_sem.at[1])
    own_p = pltpu.make_async_copy(pair_ref, pairs_ref.at[group], own_sem.at[2])
    for copy in (own, own_t, own_p):
        copy.start()

    def remote(src, dst, send, recv, target):
        return pltpu.make_async_remote_copy(
            src_ref=src, dst_ref=dst, send_sem=send, recv_sem=recv,
            device_id=target, device_id_type=MESH_ID,
        )

    def across(k, sender):
        g = others[k]
        return remote(
            out_block(g), table_ref.at[sender * QUAD + place],
            a_send.at[k], a_recv.at[sender], device(g, place),
        )

    def to_side(k, g, src, q):
        return remote(
            src, table_ref.at[g * QUAD + q], y_send.at[k], y_recv.at[k], device(group, side)
        )

    def to_core(k, g, src, q):
        return remote(
            src, table_ref.at[g * QUAD + q], c_send.at[k], c_recv.at[k], device(group, core)
        )

    def trial_copy(k, sender):
        return remote(
            trial_ref, trials_ref.at[sender], t_send.at[k], t_recv.at[sender],
            device(others[k], place),
        )

    def pair_copy(k, sender):
        return remote(
            pair_ref, pairs_ref.at[sender], p_send.at[k], p_recv.at[sender],
            device(others[k], place),
        )

    ready()
    sent = []

    def go(copy):
        copy.start()
        sent.append(copy)

    for k in range(groups - 1):
        go(across(k, group))
    go(to_side(0, group, out_block(group), place))
    go(to_core(0, group, out_block(group), place))
    for k in range(groups - 1):
        go(pair_copy(k, group))
        go(trial_copy(k, group))

    def relay(k):
        g = group if k == 0 else sources[k - 1]
        to_side(k, g, out_block(group), side).wait_recv()
        go(to_core(groups + k, g, table_ref.at[g * QUAD + side], side))

    for k in range(1, groups):
        g = sources[k - 1]
        across(k - 1, g).wait_recv()
        src = table_ref.at[g * QUAD + place]
        go(to_side(k, g, src, place))
        go(to_core(k, g, src, place))
        relay(k - 1)
    relay(groups - 1)
    far = lax.rem(core + 2, QUAD)
    for k in range(groups):
        g = group if k == 0 else sources[k - 1]
        to_core(k, g, out_block(group), core).wait_recv()
        to_core(groups + k, g, out_block(group), far).wait_recv()
    for k in range(groups - 1):
        trial_copy(k, sources[k]).wait_recv()
        pair_copy(k, sources[k]).wait_recv()
    for copy in sent:
        copy.wait_send()
    for copy in (own, own_t, own_p):
        copy.wait()


def spread(count, orbitals, trial_vectors, pair_index):
    groups = count // QUAD
    rows, grid_points = orbitals.shape
    width = grid_points // groups
    dma = pltpu.SemaphoreType.DMA
    return pl.pallas_call(
        functools.partial(spread_kernel, groups),
        out_shape=(
            jax.ShapeDtypeStruct((count, rows, width), orbitals.dtype),
            jax.ShapeDtypeStruct((groups, *trial_vectors.shape), trial_vectors.dtype),
            jax.ShapeDtypeStruct((groups, *pair_index.shape), pair_index.dtype),
        ),
        in_specs=[VMEM_SPEC] * 3,
        out_specs=(ANY_SPEC,) * 3,
        scratch_shapes=[
            dma((3,)), dma((groups,)), dma((groups,)), dma((groups,)), dma((groups,)),
            dma((2 * groups,)), dma((2 * groups,)),
            dma((groups,)), dma((groups,)), dma((groups,)), dma((groups,)),
        ],
        compiler_params=pltpu.CompilerParams(collective_id=0, has_side_effects=True),
    )(orbitals, trial_vectors, pair_index)


def density_kernel(pair_ref, trial_ref, table_ref, dens_ref, field_ref, turned):
    first_step = (pl.program_id(0) == 0) & (pl.program_id(1) == 0)

    @pl.when(first_step)
    def _():
        turned[...] = table_ref[...].T
        field_ref[...] = jnp.zeros_like(field_ref)

    index = pair_ref[0]
    is_live = jnp.max(index) >= 0

    @pl.when(is_live)
    def _():
        orbs = turned.shape[1]
        ids = lax.broadcasted_iota(jnp.int32, (orbs, index.shape[1]), 0)

        def pick(row):
            return jnp.where(ids == index[row : row + 1], 1.0, 0.0).astype(jnp.bfloat16)

        left, right = pick(0), pick(1)
        trial = trial_ref[0]
        step = min(512, turned.shape[0])
        for c in range(turned.shape[0] // step):
            rows = pl.ds(c * step, step)
            part = turned[rows, :]
            one = jnp.dot(part, left, preferred_element_type=jnp.float32)
            two = jnp.dot(part, right, preferred_element_type=jnp.float32)
            dens = (one * two).astype(jnp.bfloat16)
            dens_ref[rows, :] = dens
            field_ref[:, rows] += lax.dot_general(
                trial, dens, (((1,), (1,)), ((), ())), preferred_element_type=jnp.float32
            )

    @pl.when(jnp.logical_not(is_live))
    def _():
        dens_ref[...] = jnp.zeros_like(dens_ref)


def densities(pairs, trials, table):
    groups, batch, slots = trials.shape
    count, rows, width = table.shape
    orbs = count * rows
    block = min(512, slots)
    steps = slots // block
    return pl.pallas_call(
        density_kernel,
        grid=(groups, steps),
        out_shape=(
            jax.ShapeDtypeStruct((width, groups * slots), jnp.bfloat16),
            jax.ShapeDtypeStruct((batch, width), jnp.float32),
        ),
        in_specs=[
            pl.BlockSpec((1, 2, block), lambda g, i: (g, 0, i)),
            pl.BlockSpec((1, batch, block), lambda g, i: (g, 0, i)),
            pl.BlockSpec((orbs, width), lambda g, i: (0, 0)),
        ],
        out_specs=(
            pl.BlockSpec((width, block), lambda g, i: (0, g * steps + i)),
            pl.BlockSpec((batch, width), lambda g, i: (0, 0)),
        ),
        scratch_shapes=[pltpu.VMEM((width, orbs), jnp.bfloat16)],
    )(pairs, trials, table.reshape(orbs, width))


def split_rows(values):
    upper = values.astype(jnp.bfloat16)
    lower = (values - upper.astype(jnp.float32)).astype(jnp.bfloat16)
    return jnp.concatenate([upper, lower], 0)


def fold(stacked):
    half = stacked.shape[0] // 2
    return stacked[:half] + stacked[half:]


def apply_kernel(
    count, slabs, field_ref, scale_ref, eig_ref, dens_ref, out_ref,
    eig, dens, pieces, rs_in, slab_in, gathered, screened, potential, shares, share_in, slab_out,
    load_sem, rs_send, rs_recv, sl_send, sl_recv, ag_send, ag_recv, d_send, d_recv, o_send, o_recv,
):
    me, slab = lax.axis_index("orb"), lax.axis_index("slab")
    groups = count // QUAD
    group, place = me // QUAD, lax.rem(me, QUAD)
    batch, width = field_ref.shape
    slots = out_ref.shape[1]
    tall = pieces.shape[1]
    bands = batch // tall
    ranks = [lax.rem(me + k, count) for k in range(1, count)]
    origins = [lax.rem(me + count - k, count) for k in range(1, count)]
    layers = [lax.rem(slab + k, slabs) for k in range(1, slabs)]
    layer_from = [lax.rem(slab + slabs - k, slabs) for k in range(1, slabs)]
    ready = greet([{"orb": r} for r in ranks] + [{"slab": s} for s in layers])

    load = pltpu.make_async_copy(eig_ref.at[:, columns(group, width)], eig, load_sem.at[0])
    load.start()
    dens_loads = [
        pltpu.make_async_copy(
            dens_ref.at[:, pl.ds(g * slots, slots)], dens.at[g], load_sem.at[1 + g]
        )
        for g in range(groups)
    ]
    for copy in dens_loads:
        copy.start()

    def remote(src, dst, send, recv, target):
        return pltpu.make_async_remote_copy(
            src_ref=src, dst_ref=dst, send_sem=send, recv_sem=recv,
            device_id=target, device_id_type=MESH_ID,
        )

    sent = []

    def go(copy):
        copy.start()
        sent.append(copy)

    field = split_rows(field_ref[...])
    load.wait()
    for c in range(eig.shape[0] // LANES):
        part = fold(
            lax.dot_general(
                field, eig[pl.ds(c * LANES, LANES), :], (((1,), (1,)), ((), ())),
                preferred_element_type=jnp.float32,
            )
        )
        for h in range(bands):
            pieces[c * bands + h] = part[h * tall : (h + 1) * tall]

    def scatter(k, sender):
        return remote(
            pieces.at[ranks[k]], rs_in.at[sender], rs_send.at[k], rs_recv.at[sender],
            {"orb": ranks[k]},
        )

    def layer_copy(k, sender):
        return remote(
            slab_in.at[sender], slab_in.at[sender], sl_send.at[k], sl_recv.at[sender],
            {"slab": layers[k]},
        )

    def gather(k, sender):
        return remote(
            gathered.at[sender], gathered.at[sender], ag_send.at[k], ag_recv.at[sender],
            {"orb": ranks[k]},
        )

    ready()
    for k in range(count - 1):
        go(scatter(k, me))
    total = pieces[me]
    for k in range(count - 1):
        scatter(k, origins[k]).wait_recv()
        total = total + rs_in[origins[k]]
    slab_in[slab] = total
    for k in range(slabs - 1):
        go(layer_copy(k, slab))
    for k in range(slabs - 1):
        layer_copy(k, layer_from[k]).wait_recv()
    total = slab_in[0]
    for s in range(1, slabs):
        total = total + slab_in[s]
    gathered[me] = total
    for k in range(count - 1):
        go(gather(k, me))
    for k in range(count - 1):
        gather(k, origins[k]).wait_recv()
    for c in range(count // bands):
        rows = jnp.concatenate([gathered[c * bands + h] for h in range(bands)], 0)
        cols = slice(c * LANES, (c + 1) * LANES)
        screened[:, cols] = split_rows(rows * scale_ref[:, cols])

    for c in range(width // 256):
        cols = pl.ds(c * 256, 256)
        potential[:, cols] = split_rows(
            fold(jnp.dot(screened[...], eig[:, cols], preferred_element_type=jnp.float32))
        )

    for copy in dens_loads:
        copy.wait()

    def apply_to(g):
        @pl.loop(0, slots // 256)
        def _(c):
            cols = columns(c, 256)
            shares[g, :, cols] = fold(
                jnp.dot(potential[...], dens[g, :, cols], preferred_element_type=jnp.float32)
            )

    goals = [lax.rem(group + k, groups) for k in range(1, groups)]
    givers = [lax.rem(group + groups - k, groups) for k in range(1, groups)]

    def share_copy(k, sender):
        return remote(
            shares.at[goals[k]], share_in.at[sender], d_send.at[k], d_recv.at[sender],
            {"orb": goals[k] * QUAD + place},
        )

    def out_copy(k, sender):
        return remote(
            slab_out.at[sender], slab_out.at[sender], o_send.at[k], o_recv.at[sender],
            {"slab": layers[k]},
        )

    for k in range(groups - 1):
        apply_to(goals[k])
        go(share_copy(k, group))
    apply_to(group)
    total = shares[group]
    for k in range(groups - 1):
        share_copy(k, givers[k]).wait_recv()
        total = total + share_in[givers[k]]
    slab_out[slab] = total
    for k in range(slabs - 1):
        go(out_copy(k, slab))
    for k in range(slabs - 1):
        out_copy(k, layer_from[k]).wait_recv()
    total = slab_out[0]
    for s in range(1, slabs):
        total = total + slab_out[s]
    out_ref[...] = total
    for copy in sent:
        copy.wait_send()


def apply_direct(count, slabs, field, screening, eigenpotentials, dens, slots):
    groups = count // QUAD
    batch, width = field.shape
    neig = eigenpotentials.shape[0]
    tall = batch * neig // (count * LANES)
    dma = pltpu.SemaphoreType.DMA
    f32, b16 = jnp.float32, jnp.bfloat16
    return pl.pallas_call(
        functools.partial(apply_kernel, count, slabs),
        out_shape=jax.ShapeDtypeStruct((batch, slots), f32),
        in_specs=[VMEM_SPEC, VMEM_SPEC, ANY_SPEC, ANY_SPEC],
        out_specs=VMEM_SPEC,
        scratch_shapes=[
            pltpu.VMEM((neig, width), b16),
            pltpu.VMEM((groups, width, slots), b16),
            pltpu.VMEM((count, tall, LANES), f32),
            pltpu.VMEM((count, tall, LANES), f32),
            pltpu.VMEM((slabs, tall, LANES), f32),
            pltpu.VMEM((count, tall, LANES), f32),
            pltpu.VMEM((2 * batch, neig), b16),
            pltpu.VMEM((2 * batch, width), b16),
            pltpu.VMEM((groups, batch, slots), f32),
            pltpu.VMEM((groups, batch, slots), f32),
            pltpu.VMEM((slabs, batch, slots), f32),
            dma((1 + groups,)),
            dma((count,)), dma((count,)), dma((slabs,)), dma((slabs,)),
            dma((count,)), dma((count,)), dma((groups,)), dma((groups,)),
            dma((slabs,)), dma((slabs,)),
        ],
        compiler_params=pltpu.CompilerParams(collective_id=1, has_side_effects=True),
    )(field, screening.reshape(1, neig), eigenpotentials, dens)


def shards(count, slabs, orbitals, eigenpotentials, screening, trial_vectors, pair_index):
    table, trials, pairs = spread(count, orbitals, trial_vectors, pair_index)
    dens, field = densities(pairs, trials, table)
    slots = trial_vectors.shape[1]
    return apply_direct(count, slabs, field, screening, eigenpotentials, dens, slots)


def solution(mesh):
    return jax.shard_map(
        functools.partial(shards, mesh.shape["orb"], mesh.shape["slab"]),
        mesh=mesh,
        in_specs=(P("orb", "slab"), P(None, "slab"), P(), P(None, "orb"), P(None, "orb")),
        out_specs=P(None, "orb"),
        check_vma=False,
    )
```

```python
import functools

import jax
import jax.numpy as jnp
from jax import lax
from jax.experimental import pallas as pl
from jax.experimental.pallas import tpu as pltpu
from jax.sharding import PartitionSpec as P

QUAD = 4
LANES = 128
MESH_ID = pl.DeviceIdType.MESH
VMEM_SPEC = pl.BlockSpec(memory_space=pltpu.VMEM)
ANY_SPEC = pl.BlockSpec(memory_space=pl.ANY)


def greet(peers):
    barrier = pltpu.get_barrier_semaphore()
    for peer in peers:
        pl.semaphore_signal(barrier, inc=1, device_id=peer, device_id_type=MESH_ID)
    return lambda: pl.semaphore_wait(barrier, len(peers))


def columns(start, size):
    return pl.ds(pl.multiple_of(start * size, size), size)


def spread_kernel(
    groups, slabs, orb_hbm, trial_ref, pair_ref, table_ref, trials_ref, pairs_ref, orb_ref,
    own_sem, a_send, a_recv, y_send, y_recv, c_send, c_recv, t_send, t_recv, p_send, p_recv,
    r_send, r_recv,
):
    me, slab = lax.axis_index("orb"), lax.axis_index("slab")
    stage = pltpu.make_async_copy(orb_hbm, orb_ref, own_sem.at[3])
    stage.start()
    group, place = me // QUAD, lax.rem(me, QUAD)
    core = place + 1 - 2 * lax.rem(place, 2)
    side = lax.rem(place + 2, QUAD)
    width = table_ref.shape[2]

    def device(g, q):
        return {"orb": g * QUAD + q}

    others = [lax.rem(group + k, groups) for k in range(1, groups)]
    sources = [lax.rem(group + groups - k, groups) for k in range(1, groups)]
    layers = [lax.rem(slab + k, slabs) for k in range(1, slabs)]
    layer_from = [lax.rem(slab + slabs - k, slabs) for k in range(1, slabs)]
    ready = greet(
        [device(g, place) for g in others]
        + [device(group, core), device(group, side)]
        + [{"slab": x} for x in layers]
    )

    def out_block(g):
        return orb_ref.at[:, columns(g, width)]

    own = pltpu.make_async_copy(out_block(group), table_ref.at[me], own_sem.at[0])
    own_t = pltpu.make_async_copy(trial_ref, trials_ref.at[group], own_sem.at[1])
    own_p = pltpu.make_async_copy(pair_ref, pairs_ref.at[group], own_sem.at[2])
    own_t.start()
    own_p.start()

    def remote(src, dst, send, recv, target):
        return pltpu.make_async_remote_copy(
            src_ref=src, dst_ref=dst, send_sem=send, recv_sem=recv,
            device_id=target, device_id_type=MESH_ID,
        )

    def across(k, sender):
        g = others[k]
        return remote(
            out_block(g), table_ref.at[sender * QUAD + place],
            a_send.at[k], a_recv.at[sender], device(g, place),
        )

    def to_side(k, g, src, q):
        return remote(
            src, table_ref.at[g * QUAD + q], y_send.at[k], y_recv.at[k], device(group, side)
        )

    def to_core(k, g, src, q):
        return remote(
            src, table_ref.at[g * QUAD + q], c_send.at[k], c_recv.at[k], device(group, core)
        )

    def trial_copy(k, sender):
        return remote(
            trial_ref.at[slab], trials_ref.at[sender, slab], t_send.at[k], t_recv.at[sender],
            device(others[k], place),
        )

    def trial_relay(k, n, owner):
        part = trials_ref.at[sources[k], owner]
        slot = k * slabs + n
        return remote(part, part, r_send.at[slot], r_recv.at[slot], {"slab": layers[n]})

    def pair_copy(k, sender):
        return remote(
            pair_ref, pairs_ref.at[sender], p_send.at[k], p_recv.at[sender],
            device(others[k], place),
        )

    stage.wait()
    ready()
    sent = []

    def go(copy):
        copy.start()
        sent.append(copy)

    for k in range(groups - 1):
        go(across(k, group))
    go(to_side(0, group, out_block(group), place))
    go(to_core(0, group, out_block(group), place))
    for k in range(groups - 1):
        go(pair_copy(k, group))
        go(trial_copy(k, group))

    own.start()

    def relay(k):
        g = group if k == 0 else sources[k - 1]
        to_side(k, g, out_block(group), side).wait_recv()
        go(to_core(groups + k, g, table_ref.at[g * QUAD + side], side))

    for k in range(1, groups):
        g = sources[k - 1]
        across(k - 1, g).wait_recv()
        src = table_ref.at[g * QUAD + place]
        go(to_side(k, g, src, place))
        go(to_core(k, g, src, place))
        relay(k - 1)
    for k in range(groups - 1):
        trial_copy(k, sources[k]).wait_recv()
        for n in range(slabs - 1):
            go(trial_relay(k, n, slab))
    relay(groups - 1)
    far = lax.rem(core + 2, QUAD)
    for k in range(groups):
        g = group if k == 0 else sources[k - 1]
        to_core(k, g, out_block(group), core).wait_recv()
        to_core(groups + k, g, out_block(group), far).wait_recv()
    for k in range(groups - 1):
        pair_copy(k, sources[k]).wait_recv()
        for n in range(slabs - 1):
            trial_relay(k, n, layer_from[n]).wait_recv()
    for copy in sent:
        copy.wait_send()
    for copy in (own, own_t, own_p):
        copy.wait()


def spread(count, slabs, orbitals, trial_vectors, pair_index):
    groups = count // QUAD
    batch, slots = trial_vectors.shape
    parts = trial_vectors.reshape(slabs, batch // slabs, slots)
    rows, grid_points = orbitals.shape
    width = grid_points // groups
    dma = pltpu.SemaphoreType.DMA
    table, trials, pairs = pl.pallas_call(
        functools.partial(spread_kernel, groups, slabs),
        out_shape=(
            jax.ShapeDtypeStruct((count, rows, width), orbitals.dtype),
            jax.ShapeDtypeStruct((groups, *parts.shape), parts.dtype),
            jax.ShapeDtypeStruct((groups, *pair_index.shape), pair_index.dtype),
        ),
        in_specs=[ANY_SPEC] * 3,
        out_specs=(ANY_SPEC,) * 3,
        scratch_shapes=[
            pltpu.VMEM((rows, grid_points), orbitals.dtype),
            dma((4,)), dma((groups,)), dma((groups,)), dma((groups,)), dma((groups,)),
            dma((2 * groups,)), dma((2 * groups,)),
            dma((groups,)), dma((groups,)), dma((groups,)), dma((groups,)),
            dma((groups * slabs,)), dma((groups * slabs,)),
        ],
        compiler_params=pltpu.CompilerParams(collective_id=0, has_side_effects=True),
    )(orbitals, parts, pair_index)
    return table, trials.reshape(groups, batch, slots), pairs


def density_kernel(pair_ref, trial_ref, table_ref, dens_ref, field_ref, turned):
    first_step = (pl.program_id(0) == 0) & (pl.program_id(1) == 0)

    @pl.when(first_step)
    def _():
        turned[...] = table_ref[...].T
        field_ref[...] = jnp.zeros_like(field_ref)

    index = pair_ref[0]
    is_live = jnp.max(index) >= 0

    @pl.when(is_live)
    def _():
        orbs = turned.shape[1]
        ids = lax.broadcasted_iota(jnp.int32, (orbs, index.shape[1]), 0)

        def pick(row):
            return jnp.where(ids == index[row : row + 1], 1.0, 0.0).astype(jnp.bfloat16)

        left, right = pick(0), pick(1)
        trial = trial_ref[0]
        step = min(512, turned.shape[0])
        for c in range(turned.shape[0] // step):
            rows = pl.ds(c * step, step)
            part = turned[rows, :]
            one = jnp.dot(part, left, preferred_element_type=jnp.float32)
            two = jnp.dot(part, right, preferred_element_type=jnp.float32)
            dens = (one * two).astype(jnp.bfloat16)
            dens_ref[rows, :] = dens
            field_ref[:, rows] += lax.dot_general(
                trial, dens, (((1,), (1,)), ((), ())), preferred_element_type=jnp.float32
            )

    @pl.when(jnp.logical_not(is_live))
    def _():
        dens_ref[...] = jnp.zeros_like(dens_ref)


def densities(pairs, trials, table):
    groups, batch, slots = trials.shape
    count, rows, width = table.shape
    orbs = count * rows
    block = min(512, slots)
    steps = slots // block
    return pl.pallas_call(
        density_kernel,
        grid=(groups, steps),
        out_shape=(
            jax.ShapeDtypeStruct((width, groups * slots), jnp.bfloat16),
            jax.ShapeDtypeStruct((batch, width), jnp.float32),
        ),
        in_specs=[
            pl.BlockSpec((1, 2, block), lambda g, i: (g, 0, i)),
            pl.BlockSpec((1, batch, block), lambda g, i: (g, 0, i)),
            pl.BlockSpec((orbs, width), lambda g, i: (0, 0)),
        ],
        out_specs=(
            pl.BlockSpec((width, block), lambda g, i: (0, g * steps + i)),
            pl.BlockSpec((batch, width), lambda g, i: (0, 0)),
        ),
        scratch_shapes=[pltpu.VMEM((width, orbs), jnp.bfloat16)],
    )(pairs, trials, table.reshape(orbs, width))


def split_rows(values):
    upper = values.astype(jnp.bfloat16)
    lower = (values - upper.astype(jnp.float32)).astype(jnp.bfloat16)
    return jnp.concatenate([upper, lower], 0)


def fold(stacked):
    half = stacked.shape[0] // 2
    return stacked[:half] + stacked[half:]


def apply_kernel(
    count, slabs, spans, field_ref, scale_ref, eig_ref, dens_ref, out_ref,
    eig, dens, pieces, rs_in, slab_in, gathered, screened, potential, shares,
    load_sem, rs_send, rs_recv, sl_send, sl_recv, ag_send, ag_recv, d_send, d_recv,
):
    me, slab = lax.axis_index("orb"), lax.axis_index("slab")
    groups = count // QUAD
    group, place = me // QUAD, lax.rem(me, QUAD)
    batch, width = field_ref.shape
    slots = out_ref.shape[2]
    members = count * spans
    tall = pieces.shape[1]
    bands = batch // tall
    mine = me * slabs + slab if spans > 1 else me
    ranks = [lax.rem(mine + k, members) for k in range(1, members)]
    origins = [lax.rem(mine + members - k, members) for k in range(1, members)]
    layers = [lax.rem(slab + k, slabs) for k in range(1, slabs)]
    layer_from = [lax.rem(slab + slabs - k, slabs) for k in range(1, slabs)]
    goals = [lax.rem(group + k, groups) for k in range(1, groups)] + [group]

    def member(rank):
        if spans > 1:
            return {"orb": rank // slabs, "slab": lax.rem(rank, slabs)}
        return {"orb": rank, "slab": slab}

    def keeper(g, x):
        return {"orb": g * QUAD + place, "slab": x}

    peers = [member(r) for r in ranks]
    if spans == 1:
        peers += [keeper(g, x) for g in goals for x in layers]
    ready = greet(peers)

    load = pltpu.make_async_copy(eig_ref.at[:, columns(group, width)], eig, load_sem.at[0])
    load.start()
    dens_loads = [
        pltpu.make_async_copy(
            dens_ref.at[:, pl.ds(g * slots, slots)], dens.at[g], load_sem.at[1 + g]
        )
        for g in range(groups)
    ]
    for copy in dens_loads:
        copy.start()

    def remote(src, dst, send, recv, target):
        return pltpu.make_async_remote_copy(
            src_ref=src, dst_ref=dst, send_sem=send, recv_sem=recv,
            device_id=target, device_id_type=MESH_ID,
        )

    sent = []

    def go(copy):
        copy.start()
        sent.append(copy)

    field = split_rows(field_ref[...])
    load.wait()
    for c in range(eig.shape[0] // LANES):
        part = fold(
            lax.dot_general(
                field, eig[pl.ds(c * LANES, LANES), :], (((1,), (1,)), ((), ())),
                preferred_element_type=jnp.float32,
            )
        )
        for h in range(bands):
            pieces[c * bands + h] = part[h * tall : (h + 1) * tall]

    def scatter(k, sender):
        return remote(
            pieces.at[ranks[k]], rs_in.at[sender], rs_send.at[k], rs_recv.at[sender],
            member(ranks[k]),
        )

    def layer_copy(k, sender):
        return remote(
            slab_in.at[sender], slab_in.at[sender], sl_send.at[k], sl_recv.at[sender],
            {"slab": layers[k]},
        )

    def gather(k, sender):
        return remote(
            gathered.at[sender], gathered.at[sender], ag_send.at[k], ag_recv.at[sender],
            member(ranks[k]),
        )

    ready()
    for k in range(members - 1):
        go(scatter(k, mine))
    total = pieces[mine]
    for k in range(members - 1):
        scatter(k, origins[k]).wait_recv()
        total = total + rs_in[origins[k]]
    if spans == 1:
        slab_in[slab] = total
        for k in range(slabs - 1):
            go(layer_copy(k, slab))
        for k in range(slabs - 1):
            layer_copy(k, layer_from[k]).wait_recv()
        total = slab_in[0]
        for s in range(1, slabs):
            total = total + slab_in[s]
    gathered[mine] = total
    for k in range(members - 1):
        go(gather(k, mine))
    for k in range(members - 1):
        gather(k, origins[k]).wait_recv()
    for c in range(members // bands):
        rows = jnp.concatenate([gathered[c * bands + h] for h in range(bands)], 0)
        cols = slice(c * LANES, (c + 1) * LANES)
        screened[:, cols] = split_rows(rows * scale_ref[:, cols])

    for c in range(width // 256):
        cols = pl.ds(c * 256, 256)
        potential[:, cols] = split_rows(
            fold(jnp.dot(screened[...], eig[:, cols], preferred_element_type=jnp.float32))
        )

    for copy in dens_loads:
        copy.wait()

    def apply_to(g):
        @pl.loop(0, slots // 256)
        def _(c):
            cols = columns(c, 256)
            shares[g, :, cols] = fold(
                jnp.dot(potential[...], dens[g, :, cols], preferred_element_type=jnp.float32)
            ).astype(shares.dtype)

    givers = [lax.rem(group + groups - k, groups) for k in range(1, groups)] + [group]

    def share_copy(k, n, g, x):
        slot = k * slabs + n
        return remote(
            shares.at[goals[k]], out_ref.at[g * slabs + x], d_send.at[slot], d_recv.at[slot],
            keeper(goals[k], layers[n] if n < slabs - 1 else slab),
        )

    for k in range(groups):
        apply_to(goals[k])
        for n in range(slabs if k < groups - 1 else slabs - 1):
            go(share_copy(k, n, group, slab))
    own = pltpu.make_async_copy(
        shares.at[group], out_ref.at[group * slabs + slab], load_sem.at[0]
    )
    own.start()
    for k in range(groups):
        for n in range(slabs if k < groups - 1 else slabs - 1):
            share_copy(k, n, givers[k], layer_from[n] if n < slabs - 1 else slab).wait_recv()
    own.wait()
    for copy in sent:
        copy.wait_send()


def apply_direct(count, slabs, field, screening, eigenpotentials, dens, slots):
    groups = count // QUAD
    batch, width = field.shape
    neig = eigenpotentials.shape[0]
    spans = slabs if batch * neig % (count * slabs * LANES) == 0 else 1
    members = count * spans
    tall = batch * neig // (members * LANES)
    dma = pltpu.SemaphoreType.DMA
    f32, b16 = jnp.float32, jnp.bfloat16
    parts = pl.pallas_call(
        functools.partial(apply_kernel, count, slabs, spans),
        out_shape=jax.ShapeDtypeStruct((groups * slabs, batch, slots), b16),
        in_specs=[VMEM_SPEC, VMEM_SPEC, ANY_SPEC, ANY_SPEC],
        out_specs=ANY_SPEC,
        scratch_shapes=[
            pltpu.VMEM((neig, width), b16),
            pltpu.VMEM((groups, width, slots), b16),
            pltpu.VMEM((members, tall, LANES), f32),
            pltpu.VMEM((members, tall, LANES), f32),
            pltpu.VMEM((slabs, tall, LANES), f32),
            pltpu.VMEM((members, tall, LANES), f32),
            pltpu.VMEM((2 * batch, neig), b16),
            pltpu.VMEM((2 * batch, width), b16),
            pltpu.VMEM((groups, batch, slots), b16),
            dma((1 + groups,)),
            dma((members,)), dma((members,)), dma((slabs,)), dma((slabs,)),
            dma((members,)), dma((members,)),
            dma((groups * slabs,)), dma((groups * slabs,)),
        ],
        compiler_params=pltpu.CompilerParams(collective_id=1, has_side_effects=True),
    )(field, screening.reshape(1, neig), eigenpotentials, dens)
    return jnp.sum(parts.astype(f32), 0)


def shards(count, slabs, orbitals, eigenpotentials, screening, trial_vectors, pair_index):
    table, trials, pairs = spread(count, slabs, orbitals, trial_vectors, pair_index)
    dens, field = densities(pairs, trials, table)
    slots = trial_vectors.shape[1]
    return apply_direct(count, slabs, field, screening, eigenpotentials, dens, slots)


def solution(mesh):
    return jax.shard_map(
        functools.partial(shards, mesh.shape["orb"], mesh.shape["slab"]),
        mesh=mesh,
        in_specs=(P("orb", "slab"), P(None, "slab"), P(), P(None, "orb"), P(None, "orb")),
        out_specs=P(None, "orb"),
        check_vma=False,
    )
```

```python
import functools

import jax
import jax.numpy as jnp
from jax import lax
from jax.experimental import pallas as pl
from jax.experimental.pallas import tpu as pltpu
from jax.sharding import PartitionSpec as P

QUAD = 4
LANES = 128
MESH_ID = pl.DeviceIdType.MESH
VMEM_SPEC = pl.BlockSpec(memory_space=pltpu.VMEM)
ANY_SPEC = pl.BlockSpec(memory_space=pl.ANY)


def greet(peers):
    barrier = pltpu.get_barrier_semaphore()
    for peer in peers:
        pl.semaphore_signal(barrier, inc=1, device_id=peer, device_id_type=MESH_ID)
    return lambda: pl.semaphore_wait(barrier, len(peers))


def flip(index, mask, extent):
    total, bit = 0, 1
    while bit < extent:
        digit = lax.rem(index // bit, 2)
        total = total + bit * (1 - digit if mask & bit else digit)
        bit *= 2
    return total


def columns(start, size):
    return pl.ds(pl.multiple_of(start * size, size), size)


def spread_kernel(
    groups, slabs, orb_hbm, trial_ref, pair_ref, table_ref, trials_ref, pairs_ref, orb_ref,
    own_sem, a_send, a_recv, y_send, y_recv, c_send, c_recv, t_send, t_recv, p_send, p_recv,
    r_send, r_recv,
):
    me, slab = lax.axis_index("orb"), lax.axis_index("slab")
    stage = pltpu.make_async_copy(orb_hbm, orb_ref, own_sem.at[3])
    stage.start()
    group, place = me // QUAD, lax.rem(me, QUAD)
    core = place + 1 - 2 * lax.rem(place, 2)
    side = lax.rem(place + 2, QUAD)
    width = table_ref.shape[2]

    def device(g, q):
        return {"orb": g * QUAD + q}

    others = [flip(group, k, groups) for k in range(groups - 1, 0, -1)]
    sources = others
    layers = [lax.rem(slab + k, slabs) for k in range(1, slabs)]
    layer_from = [lax.rem(slab + slabs - k, slabs) for k in range(1, slabs)]
    ready = greet(
        [device(g, place) for g in others]
        + [device(group, core), device(group, side)]
        + [{"slab": x} for x in layers]
    )

    def out_block(g):
        return orb_ref.at[:, columns(g, width)]

    own = pltpu.make_async_copy(out_block(group), table_ref.at[me], own_sem.at[0])
    own_t = pltpu.make_async_copy(trial_ref, trials_ref.at[group], own_sem.at[1])
    own_p = pltpu.make_async_copy(pair_ref, pairs_ref.at[group], own_sem.at[2])
    own_t.start()
    own_p.start()

    def remote(src, dst, send, recv, target):
        return pltpu.make_async_remote_copy(
            src_ref=src, dst_ref=dst, send_sem=send, recv_sem=recv,
            device_id=target, device_id_type=MESH_ID,
        )

    def across(k, sender):
        g = others[k]
        return remote(
            out_block(g), table_ref.at[sender * QUAD + place],
            a_send.at[k], a_recv.at[sender], device(g, place),
        )

    def to_side(k, g, src, q):
        return remote(
            src, table_ref.at[g * QUAD + q], y_send.at[k], y_recv.at[k], device(group, side)
        )

    def to_core(k, g, src, q):
        return remote(
            src, table_ref.at[g * QUAD + q], c_send.at[k], c_recv.at[k], device(group, core)
        )

    def trial_copy(k, sender):
        return remote(
            trial_ref.at[slab], trials_ref.at[sender, slab], t_send.at[k], t_recv.at[sender],
            device(others[k], place),
        )

    def trial_relay(k, n, owner):
        part = trials_ref.at[sources[k], owner]
        slot = k * slabs + n
        return remote(part, part, r_send.at[slot], r_recv.at[slot], {"slab": layers[n]})

    def pair_copy(k, sender):
        return remote(
            pair_ref, pairs_ref.at[sender], p_send.at[k], p_recv.at[sender],
            device(others[k], place),
        )

    stage.wait()
    ready()
    sent = []

    def go(copy):
        copy.start()
        sent.append(copy)

    for k in range(groups - 1):
        go(across(k, group))
    go(to_side(0, group, out_block(group), place))
    go(to_core(0, group, out_block(group), place))
    for k in range(groups - 1):
        go(pair_copy(k, group))
        go(trial_copy(k, group))

    own.start()

    def relay(k):
        g = group if k == 0 else sources[k - 1]
        to_side(k, g, out_block(group), side).wait_recv()
        go(to_core(groups + k, g, table_ref.at[g * QUAD + side], side))

    for k in range(1, groups):
        g = sources[k - 1]
        across(k - 1, g).wait_recv()
        src = table_ref.at[g * QUAD + place]
        go(to_side(k, g, src, place))
        go(to_core(k, g, src, place))
        relay(k - 1)
    for k in range(groups - 1):
        trial_copy(k, sources[k]).wait_recv()
        for n in range(slabs - 1):
            go(trial_relay(k, n, slab))
    relay(groups - 1)
    far = lax.rem(core + 2, QUAD)
    for k in range(groups):
        g = group if k == 0 else sources[k - 1]
        to_core(k, g, out_block(group), core).wait_recv()
        to_core(groups + k, g, out_block(group), far).wait_recv()
    for k in range(groups - 1):
        pair_copy(k, sources[k]).wait_recv()
        for n in range(slabs - 1):
            trial_relay(k, n, layer_from[n]).wait_recv()
    for copy in sent:
        copy.wait_send()
    for copy in (own, own_t, own_p):
        copy.wait()


def spread(count, slabs, orbitals, trial_vectors, pair_index):
    groups = count // QUAD
    batch, slots = trial_vectors.shape
    parts = trial_vectors.reshape(slabs, batch // slabs, slots)
    rows, grid_points = orbitals.shape
    width = grid_points // groups
    dma = pltpu.SemaphoreType.DMA
    table, trials, pairs = pl.pallas_call(
        functools.partial(spread_kernel, groups, slabs),
        out_shape=(
            jax.ShapeDtypeStruct((count, rows, width), orbitals.dtype),
            jax.ShapeDtypeStruct((groups, *parts.shape), parts.dtype),
            jax.ShapeDtypeStruct((groups, *pair_index.shape), pair_index.dtype),
        ),
        in_specs=[ANY_SPEC] * 3,
        out_specs=(ANY_SPEC,) * 3,
        scratch_shapes=[
            pltpu.VMEM((rows, grid_points), orbitals.dtype),
            dma((4,)), dma((groups,)), dma((groups,)), dma((groups,)), dma((groups,)),
            dma((2 * groups,)), dma((2 * groups,)),
            dma((groups,)), dma((groups,)), dma((groups,)), dma((groups,)),
            dma((groups * slabs,)), dma((groups * slabs,)),
        ],
        compiler_params=pltpu.CompilerParams(collective_id=0, has_side_effects=True),
    )(orbitals, parts, pair_index)
    return table, trials.reshape(groups, batch, slots), pairs


def density_kernel(pair_ref, trial_ref, table_ref, dens_ref, field_ref, turned):
    first_step = (pl.program_id(0) == 0) & (pl.program_id(1) == 0)

    @pl.when(first_step)
    def _():
        turned[...] = table_ref[...].T
        field_ref[...] = jnp.zeros_like(field_ref)

    index = pair_ref[0]
    is_live = jnp.max(index) >= 0

    @pl.when(is_live)
    def _():
        orbs = turned.shape[1]
        ids = lax.broadcasted_iota(jnp.int32, (orbs, index.shape[1]), 0)

        def pick(row):
            return jnp.where(ids == index[row : row + 1], 1.0, 0.0).astype(jnp.bfloat16)

        left, right = pick(0), pick(1)
        trial = trial_ref[0]
        step = min(512, turned.shape[0])
        for c in range(turned.shape[0] // step):
            rows = pl.ds(c * step, step)
            part = turned[rows, :]
            one = jnp.dot(part, left, preferred_element_type=jnp.float32)
            two = jnp.dot(part, right, preferred_element_type=jnp.float32)
            dens = (one * two).astype(jnp.bfloat16)
            dens_ref[rows, :] = dens
            field_ref[:, rows] += lax.dot_general(
                trial, dens, (((1,), (1,)), ((), ())), preferred_element_type=jnp.float32
            )

    @pl.when(jnp.logical_not(is_live))
    def _():
        dens_ref[...] = jnp.zeros_like(dens_ref)


def densities(pairs, trials, table):
    groups, batch, slots = trials.shape
    count, rows, width = table.shape
    orbs = count * rows
    block = min(512, slots)
    steps = slots // block
    return pl.pallas_call(
        density_kernel,
        grid=(groups, steps),
        out_shape=(
            jax.ShapeDtypeStruct((width, groups * slots), jnp.bfloat16),
            jax.ShapeDtypeStruct((batch, width), jnp.float32),
        ),
        in_specs=[
            pl.BlockSpec((1, 2, block), lambda g, i: (g, 0, i)),
            pl.BlockSpec((1, batch, block), lambda g, i: (g, 0, i)),
            pl.BlockSpec((orbs, width), lambda g, i: (0, 0)),
        ],
        out_specs=(
            pl.BlockSpec((width, block), lambda g, i: (0, g * steps + i)),
            pl.BlockSpec((batch, width), lambda g, i: (0, 0)),
        ),
        scratch_shapes=[pltpu.VMEM((width, orbs), jnp.bfloat16)],
    )(pairs, trials, table.reshape(orbs, width))


def split_rows(values):
    upper = values.astype(jnp.bfloat16)
    lower = (values - upper.astype(jnp.float32)).astype(jnp.bfloat16)
    return jnp.concatenate([upper, lower], 0)


def fold(stacked):
    half = stacked.shape[0] // 2
    return stacked[:half] + stacked[half:]


def apply_kernel(
    count, slabs, field_ref, scale_ref, eig_ref, dens_ref, out_ref,
    eig, dens, pieces, rs_in, outer_in, gathered, screened, potential, shares,
    load_sem, rs_send, rs_recv, z_send, z_recv, ag_send, ag_recv, d_send, d_recv,
):
    me, slab = lax.axis_index("orb"), lax.axis_index("slab")
    groups = count // QUAD
    group, place = me // QUAD, lax.rem(me, QUAD)
    batch, width = field_ref.shape
    slots = out_ref.shape[2]
    members = QUAD * slabs
    tall = pieces.shape[1]
    bands = batch // tall
    mine = place * slabs + slab
    ranks = [lax.rem(mine + k, members) for k in range(1, members)]
    origins = [lax.rem(mine + members - k, members) for k in range(1, members)]
    layers = [lax.rem(slab + k, slabs) for k in range(1, slabs)]
    layer_from = [lax.rem(slab + slabs - k, slabs) for k in range(1, slabs)]
    outers = [flip(group, k, groups) for k in range(groups - 1, 0, -1)]
    goals = outers + [group]

    def member(rank):
        return {"orb": group * QUAD + rank // slabs, "slab": lax.rem(rank, slabs)}

    def keeper(g, x):
        return {"orb": g * QUAD + place, "slab": x}

    peers = [member(r) for r in ranks]
    peers += [keeper(g, x) for g in outers for x in layers + [slab]]
    ready = greet(peers)

    load = pltpu.make_async_copy(eig_ref.at[:, columns(group, width)], eig, load_sem.at[0])
    load.start()
    dens_loads = [
        pltpu.make_async_copy(
            dens_ref.at[:, pl.ds(g * slots, slots)], dens.at[g], load_sem.at[1 + g]
        )
        for g in range(groups)
    ]
    for copy in dens_loads:
        copy.start()

    def remote(src, dst, send, recv, target):
        return pltpu.make_async_remote_copy(
            src_ref=src, dst_ref=dst, send_sem=send, recv_sem=recv,
            device_id=target, device_id_type=MESH_ID,
        )

    sent = []

    def go(copy):
        copy.start()
        sent.append(copy)

    field = split_rows(field_ref[...])
    load.wait()
    for c in range(eig.shape[0] // LANES):
        part = fold(
            lax.dot_general(
                field, eig[pl.ds(c * LANES, LANES), :], (((1,), (1,)), ((), ())),
                preferred_element_type=jnp.float32,
            )
        )
        for h in range(bands):
            pieces[c * bands + h] = part[h * tall : (h + 1) * tall]

    def scatter(k, sender):
        return remote(
            pieces.at[ranks[k]], rs_in.at[sender], rs_send.at[k], rs_recv.at[sender],
            member(ranks[k]),
        )

    def outer_copy(k, sender):
        return remote(
            outer_in.at[sender], outer_in.at[sender], z_send.at[k], z_recv.at[k],
            keeper(outers[k], slab),
        )

    def gather(k, sender):
        return remote(
            gathered.at[sender], gathered.at[sender], ag_send.at[k], ag_recv.at[sender],
            member(ranks[k]),
        )

    ready()
    for k in range(members - 1):
        go(scatter(k, mine))
    total = pieces[mine]
    for k in range(members - 1):
        scatter(k, origins[k]).wait_recv()
        total = total + rs_in[origins[k]]
    outer_in[group] = total
    for k in range(groups - 1):
        go(outer_copy(k, group))
    for k in range(groups - 1):
        outer_copy(k, outers[k]).wait_recv()
    total = outer_in[0]
    for g in range(1, groups):
        total = total + outer_in[g]
    gathered[mine] = total
    for k in range(members - 1):
        go(gather(k, mine))
    for k in range(members - 1):
        gather(k, origins[k]).wait_recv()
    for c in range(members // bands):
        rows = jnp.concatenate([gathered[c * bands + h] for h in range(bands)], 0)
        cols = slice(c * LANES, (c + 1) * LANES)
        screened[:, cols] = split_rows(rows * scale_ref[:, cols])

    for c in range(width // 256):
        cols = pl.ds(c * 256, 256)
        potential[:, cols] = split_rows(
            fold(jnp.dot(screened[...], eig[:, cols], preferred_element_type=jnp.float32))
        )

    for copy in dens_loads:
        copy.wait()

    def apply_to(g):
        @pl.loop(0, slots // 256)
        def _(c):
            cols = columns(c, 256)
            shares[g, :, cols] = fold(
                jnp.dot(potential[...], dens[g, :, cols], preferred_element_type=jnp.float32)
            ).astype(shares.dtype)

    def share_copy(k, n, g, x):
        slot = k * slabs + n
        return remote(
            shares.at[goals[k]], out_ref.at[g * slabs + x], d_send.at[slot], d_recv.at[slot],
            keeper(goals[k], layers[n] if n < slabs - 1 else slab),
        )

    for k in range(groups):
        apply_to(goals[k])
        for n in range(slabs if k < groups - 1 else slabs - 1):
            go(share_copy(k, n, group, slab))
    own = pltpu.make_async_copy(
        shares.at[group], out_ref.at[group * slabs + slab], load_sem.at[0]
    )
    own.start()
    for k in range(groups):
        for n in range(slabs if k < groups - 1 else slabs - 1):
            share_copy(k, n, goals[k], layer_from[n] if n < slabs - 1 else slab).wait_recv()
    own.wait()
    for copy in sent:
        copy.wait_send()


def apply_direct(count, slabs, field, screening, eigenpotentials, dens, slots):
    groups = count // QUAD
    batch, width = field.shape
    neig = eigenpotentials.shape[0]
    members = QUAD * slabs
    tall = batch * neig // (members * LANES)
    dma = pltpu.SemaphoreType.DMA
    f32, b16 = jnp.float32, jnp.bfloat16
    parts = pl.pallas_call(
        functools.partial(apply_kernel, count, slabs),
        out_shape=jax.ShapeDtypeStruct((groups * slabs, batch, slots), b16),
        in_specs=[VMEM_SPEC, VMEM_SPEC, ANY_SPEC, ANY_SPEC],
        out_specs=ANY_SPEC,
        scratch_shapes=[
            pltpu.VMEM((neig, width), b16),
            pltpu.VMEM((groups, width, slots), b16),
            pltpu.VMEM((members, tall, LANES), f32),
            pltpu.VMEM((members, tall, LANES), f32),
            pltpu.VMEM((groups, tall, LANES), f32),
            pltpu.VMEM((members, tall, LANES), f32),
            pltpu.VMEM((2 * batch, neig), b16),
            pltpu.VMEM((2 * batch, width), b16),
            pltpu.VMEM((groups, batch, slots), b16),
            dma((1 + groups,)),
            dma((members,)), dma((members,)), dma((groups,)), dma((groups,)),
            dma((members,)), dma((members,)),
            dma((groups * slabs,)), dma((groups * slabs,)),
        ],
        compiler_params=pltpu.CompilerParams(collective_id=1, has_side_effects=True),
    )(field, screening.reshape(1, neig), eigenpotentials, dens)
    return jnp.sum(parts.astype(f32), 0)


def shards(count, slabs, orbitals, eigenpotentials, screening, trial_vectors, pair_index):
    table, trials, pairs = spread(count, slabs, orbitals, trial_vectors, pair_index)
    dens, field = densities(pairs, trials, table)
    slots = trial_vectors.shape[1]
    return apply_direct(count, slabs, field, screening, eigenpotentials, dens, slots)


def solution(mesh):
    return jax.shard_map(
        functools.partial(shards, mesh.shape["orb"], mesh.shape["slab"]),
        mesh=mesh,
        in_specs=(P("orb", "slab"), P(None, "slab"), P(), P(None, "orb"), P(None, "orb")),
        out_specs=P(None, "orb"),
        check_vma=False,
    )
```

```python
import functools

import jax
import jax.numpy as jnp
from jax import lax
from jax.experimental import pallas as pl
from jax.experimental.pallas import tpu as pltpu
from jax.sharding import PartitionSpec as P

QUAD = 4
LANES = 128
MESH_ID = pl.DeviceIdType.MESH
VMEM_SPEC = pl.BlockSpec(memory_space=pltpu.VMEM)
ANY_SPEC = pl.BlockSpec(memory_space=pl.ANY)


def greet(peers):
    barrier = pltpu.get_barrier_semaphore()
    for peer in peers:
        pl.semaphore_signal(barrier, inc=1, device_id=peer, device_id_type=MESH_ID)
    return lambda: pl.semaphore_wait(barrier, len(peers))


def flip(index, mask, extent):
    total, bit = 0, 1
    while bit < extent:
        digit = lax.rem(index // bit, 2)
        total = total + bit * (1 - digit if mask & bit else digit)
        bit *= 2
    return total


def columns(start, size):
    return pl.ds(pl.multiple_of(start * size, size), size)


def spread_kernel(
    groups, slabs, orb_hbm, trial_ref, pair_ref, table_ref, trials_ref, pairs_ref, orb_ref,
    own_sem, a_send, a_recv, y_send, y_recv, c_send, c_recv, t_send, t_recv, p_send, p_recv,
    r_send, r_recv,
):
    me, slab = lax.axis_index("orb"), lax.axis_index("slab")
    stage = pltpu.make_async_copy(orb_hbm, orb_ref, own_sem.at[3])
    stage.start()
    group, place = me // QUAD, lax.rem(me, QUAD)
    core = place + 1 - 2 * lax.rem(place, 2)
    side = lax.rem(place + 2, QUAD)
    width = table_ref.shape[2]

    def device(g, q):
        return {"orb": g * QUAD + q}

    others = [lax.rem(group + k, groups) for k in range(1, groups)]
    sources = [lax.rem(group + groups - k, groups) for k in range(1, groups)]
    layers = [lax.rem(slab + k, slabs) for k in range(1, slabs)]
    layer_from = [lax.rem(slab + slabs - k, slabs) for k in range(1, slabs)]
    ready = greet(
        [device(g, place) for g in others]
        + [device(group, core), device(group, side)]
        + [{"slab": x} for x in layers]
    )

    def out_block(g):
        return orb_ref.at[:, columns(g, width)]

    own = pltpu.make_async_copy(out_block(group), table_ref.at[me], own_sem.at[0])
    own_t = pltpu.make_async_copy(trial_ref, trials_ref.at[group], own_sem.at[1])
    own_p = pltpu.make_async_copy(pair_ref, pairs_ref.at[group], own_sem.at[2])
    own_t.start()
    own_p.start()

    def remote(src, dst, send, recv, target):
        return pltpu.make_async_remote_copy(
            src_ref=src, dst_ref=dst, send_sem=send, recv_sem=recv,
            device_id=target, device_id_type=MESH_ID,
        )

    def across(k, sender):
        g = others[k]
        return remote(
            out_block(g), table_ref.at[sender * QUAD + place],
            a_send.at[k], a_recv.at[sender], device(g, place),
        )

    def to_side(k, g, src, q):
        return remote(
            src, table_ref.at[g * QUAD + q], y_send.at[k], y_recv.at[k], device(group, side)
        )

    def to_core(k, g, src, q):
        return remote(
            src, table_ref.at[g * QUAD + q], c_send.at[k], c_recv.at[k], device(group, core)
        )

    def trial_copy(k, sender):
        return remote(
            trial_ref.at[slab], trials_ref.at[sender, slab], t_send.at[k], t_recv.at[sender],
            device(others[k], place),
        )

    def trial_relay(k, n, owner):
        part = trials_ref.at[sources[k], owner]
        slot = k * slabs + n
        return remote(part, part, r_send.at[slot], r_recv.at[slot], {"slab": layers[n]})

    def pair_copy(k, sender):
        return remote(
            pair_ref, pairs_ref.at[sender], p_send.at[k], p_recv.at[sender],
            device(others[k], place),
        )

    stage.wait()
    ready()
    sent = []

    def go(copy):
        copy.start()
        sent.append(copy)

    for k in range(groups - 1):
        go(across(k, group))
    go(to_side(0, group, out_block(group), place))
    go(to_core(0, group, out_block(group), place))
    for k in range(groups - 1):
        go(pair_copy(k, group))
        go(trial_copy(k, group))

    own.start()

    def relay(k):
        g = group if k == 0 else sources[k - 1]
        to_side(k, g, out_block(group), side).wait_recv()
        go(to_core(groups + k, g, table_ref.at[g * QUAD + side], side))

    for k in range(1, groups):
        g = sources[k - 1]
        across(k - 1, g).wait_recv()
        src = table_ref.at[g * QUAD + place]
        go(to_side(k, g, src, place))
        go(to_core(k, g, src, place))
        relay(k - 1)
    for k in range(groups - 1):
        trial_copy(k, sources[k]).wait_recv()
        for n in range(slabs - 1):
            go(trial_relay(k, n, slab))
    relay(groups - 1)
    far = lax.rem(core + 2, QUAD)
    for k in range(groups):
        g = group if k == 0 else sources[k - 1]
        to_core(k, g, out_block(group), core).wait_recv()
        to_core(groups + k, g, out_block(group), far).wait_recv()
    for k in range(groups - 1):
        pair_copy(k, sources[k]).wait_recv()
        for n in range(slabs - 1):
            trial_relay(k, n, layer_from[n]).wait_recv()
    for copy in sent:
        copy.wait_send()
    for copy in (own, own_t, own_p):
        copy.wait()


def spread(count, slabs, orbitals, trial_vectors, pair_index):
    groups = count // QUAD
    batch, slots = trial_vectors.shape
    parts = trial_vectors.reshape(slabs, batch // slabs, slots)
    rows, grid_points = orbitals.shape
    width = grid_points // groups
    dma = pltpu.SemaphoreType.DMA
    table, trials, pairs = pl.pallas_call(
        functools.partial(spread_kernel, groups, slabs),
        out_shape=(
            jax.ShapeDtypeStruct((count, rows, width), orbitals.dtype),
            jax.ShapeDtypeStruct((groups, *parts.shape), parts.dtype),
            jax.ShapeDtypeStruct((groups, *pair_index.shape), pair_index.dtype),
        ),
        in_specs=[ANY_SPEC] * 3,
        out_specs=(ANY_SPEC,) * 3,
        scratch_shapes=[
            pltpu.VMEM((rows, grid_points), orbitals.dtype),
            dma((4,)), dma((groups,)), dma((groups,)), dma((groups,)), dma((groups,)),
            dma((2 * groups,)), dma((2 * groups,)),
            dma((groups,)), dma((groups,)), dma((groups,)), dma((groups,)),
            dma((groups * slabs,)), dma((groups * slabs,)),
        ],
        compiler_params=pltpu.CompilerParams(collective_id=0, has_side_effects=True),
    )(orbitals, parts, pair_index)
    return table, trials.reshape(groups, batch, slots), pairs


def density_kernel(pair_ref, trial_ref, table_ref, dens_ref, field_ref, turned, blocks, sems):
    count, width, block = blocks.shape
    steps = trial_ref.shape[2] // block
    orbs = turned.shape[1]
    turned[...] = table_ref[...].T
    field_ref[...] = jnp.zeros_like(field_ref)

    def block_index(b):
        return pair_ref[b // steps, :, columns(lax.rem(b, steps), block)]

    def write_out(b):
        return pltpu.make_async_copy(blocks.at[b], dens_ref.at[:, columns(b, block)], sems.at[b])

    @pl.loop(0, count)
    def _(b):
        index = block_index(b)

        @pl.when(jnp.max(index) >= 0)
        def _():
            ids = lax.broadcasted_iota(jnp.int32, (orbs, block), 0)

            def pick(row):
                return jnp.where(ids == index[row : row + 1], 1.0, 0.0).astype(jnp.bfloat16)

            left, right = pick(0), pick(1)
            trial = trial_ref[b // steps, :, columns(lax.rem(b, steps), block)]
            step = min(512, width)
            for c in range(width // step):
                rows = pl.ds(c * step, step)
                part = turned[rows, :]
                one = jnp.dot(part, left, preferred_element_type=jnp.float32)
                two = jnp.dot(part, right, preferred_element_type=jnp.float32)
                dens = (one * two).astype(jnp.bfloat16)
                blocks[b, rows, :] = dens
                field_ref[:, rows] += lax.dot_general(
                    trial, dens, (((1,), (1,)), ((), ())), preferred_element_type=jnp.float32
                )
            write_out(b).start()

    @pl.loop(0, count)
    def _(b):
        @pl.when(jnp.max(block_index(b)) >= 0)
        def _():
            write_out(b).wait()


def densities(pairs, trials, table):
    groups, batch, slots = trials.shape
    count, rows, width = table.shape
    orbs = count * rows
    block = min(512, slots)
    blocks = groups * slots // block
    return pl.pallas_call(
        density_kernel,
        out_shape=(
            jax.ShapeDtypeStruct((width, groups * slots), jnp.bfloat16),
            jax.ShapeDtypeStruct((batch, width), jnp.float32),
        ),
        in_specs=[VMEM_SPEC] * 3,
        out_specs=(ANY_SPEC, VMEM_SPEC),
        scratch_shapes=[
            pltpu.VMEM((width, orbs), jnp.bfloat16),
            pltpu.VMEM((blocks, width, block), jnp.bfloat16),
            pltpu.SemaphoreType.DMA((blocks,)),
        ],
    )(pairs, trials, table.reshape(orbs, width))


def split_rows(values):
    upper = values.astype(jnp.bfloat16)
    lower = (values - upper.astype(jnp.float32)).astype(jnp.bfloat16)
    return jnp.concatenate([upper, lower], 0)


def fold(stacked):
    half = stacked.shape[0] // 2
    return stacked[:half] + stacked[half:]


def apply_kernel(
    count, slabs, field_ref, scale_ref, eig_ref, dens_ref, out_ref,
    eig, dens, pieces, rs_in, outer_in, gathered, screened, potential, shares,
    load_sem, rs_send, rs_recv, z_send, z_recv, ag_send, ag_recv, d_send, d_recv,
):
    me, slab = lax.axis_index("orb"), lax.axis_index("slab")
    groups = count // QUAD
    group, place = me // QUAD, lax.rem(me, QUAD)
    batch, width = field_ref.shape
    slots = out_ref.shape[2]
    members = QUAD * slabs
    tall = pieces.shape[1]
    bands = batch // tall
    mine = place * slabs + slab
    ranks = [lax.rem(mine + k, members) for k in range(1, members)]
    origins = [lax.rem(mine + members - k, members) for k in range(1, members)]
    layers = [lax.rem(slab + k, slabs) for k in range(1, slabs)]
    layer_from = [lax.rem(slab + slabs - k, slabs) for k in range(1, slabs)]
    outers = [flip(group, k, groups) for k in range(groups - 1, 0, -1)]
    goals = outers + [group]

    def member(rank):
        return {"orb": group * QUAD + rank // slabs, "slab": lax.rem(rank, slabs)}

    def keeper(g, x):
        return {"orb": g * QUAD + place, "slab": x}

    peers = [member(r) for r in ranks]
    peers += [keeper(g, x) for g in outers for x in layers + [slab]]
    ready = greet(peers)

    load = pltpu.make_async_copy(eig_ref.at[:, columns(group, width)], eig, load_sem.at[0])
    load.start()
    dens_loads = [
        pltpu.make_async_copy(
            dens_ref.at[:, pl.ds(g * slots, slots)], dens.at[g], load_sem.at[1 + g]
        )
        for g in range(groups)
    ]
    for copy in dens_loads:
        copy.start()

    def remote(src, dst, send, recv, target):
        return pltpu.make_async_remote_copy(
            src_ref=src, dst_ref=dst, send_sem=send, recv_sem=recv,
            device_id=target, device_id_type=MESH_ID,
        )

    sent = []

    def go(copy):
        copy.start()
        sent.append(copy)

    field = split_rows(field_ref[...])
    load.wait()
    for c in range(eig.shape[0] // LANES):
        part = fold(
            lax.dot_general(
                field, eig[pl.ds(c * LANES, LANES), :], (((1,), (1,)), ((), ())),
                preferred_element_type=jnp.float32,
            )
        )
        for h in range(bands):
            pieces[c * bands + h] = part[h * tall : (h + 1) * tall]

    def scatter(k, sender):
        return remote(
            pieces.at[ranks[k]], rs_in.at[sender], rs_send.at[k], rs_recv.at[sender],
            member(ranks[k]),
        )

    def outer_copy(k, sender):
        return remote(
            outer_in.at[sender], outer_in.at[sender], z_send.at[k], z_recv.at[k],
            keeper(outers[k], slab),
        )

    def gather(k, sender):
        return remote(
            gathered.at[sender], gathered.at[sender], ag_send.at[k], ag_recv.at[sender],
            member(ranks[k]),
        )

    ready()
    for k in range(members - 1):
        go(scatter(k, mine))
    total = pieces[mine]
    for k in range(members - 1):
        scatter(k, origins[k]).wait_recv()
        total = total + rs_in[origins[k]]
    outer_in[group] = total
    for k in range(groups - 1):
        go(outer_copy(k, group))
    for k in range(groups - 1):
        outer_copy(k, outers[k]).wait_recv()
    total = outer_in[0]
    for g in range(1, groups):
        total = total + outer_in[g]
    gathered[mine] = total
    for k in range(members - 1):
        go(gather(k, mine))
    for k in range(members - 1):
        gather(k, origins[k]).wait_recv()
    for c in range(members // bands):
        rows = jnp.concatenate([gathered[c * bands + h] for h in range(bands)], 0)
        cols = slice(c * LANES, (c + 1) * LANES)
        screened[:, cols] = split_rows(rows * scale_ref[:, cols])

    for c in range(width // 256):
        cols = pl.ds(c * 256, 256)
        potential[:, cols] = split_rows(
            fold(jnp.dot(screened[...], eig[:, cols], preferred_element_type=jnp.float32))
        )

    for copy in dens_loads:
        copy.wait()

    def apply_to(g):
        @pl.loop(0, slots // 256)
        def _(c):
            cols = columns(c, 256)
            shares[g, :, cols] = fold(
                jnp.dot(potential[...], dens[g, :, cols], preferred_element_type=jnp.float32)
            ).astype(shares.dtype)

    def share_copy(k, n, g, x):
        slot = k * slabs + n
        return remote(
            shares.at[goals[k]], out_ref.at[g * slabs + x], d_send.at[slot], d_recv.at[slot],
            keeper(goals[k], layers[n] if n < slabs - 1 else slab),
        )

    for k in range(groups):
        apply_to(goals[k])
        for n in range(slabs if k < groups - 1 else slabs - 1):
            go(share_copy(k, n, group, slab))
    own = pltpu.make_async_copy(
        shares.at[group], out_ref.at[group * slabs + slab], load_sem.at[0]
    )
    own.start()
    for k in range(groups):
        for n in range(slabs if k < groups - 1 else slabs - 1):
            share_copy(k, n, goals[k], layer_from[n] if n < slabs - 1 else slab).wait_recv()
    own.wait()
    for copy in sent:
        copy.wait_send()


def apply_direct(count, slabs, field, screening, eigenpotentials, dens, slots):
    groups = count // QUAD
    batch, width = field.shape
    neig = eigenpotentials.shape[0]
    members = QUAD * slabs
    tall = batch * neig // (members * LANES)
    dma = pltpu.SemaphoreType.DMA
    f32, b16 = jnp.float32, jnp.bfloat16
    parts = pl.pallas_call(
        functools.partial(apply_kernel, count, slabs),
        out_shape=jax.ShapeDtypeStruct((groups * slabs, batch, slots), b16),
        in_specs=[VMEM_SPEC, VMEM_SPEC, ANY_SPEC, ANY_SPEC],
        out_specs=ANY_SPEC,
        scratch_shapes=[
            pltpu.VMEM((neig, width), b16),
            pltpu.VMEM((groups, width, slots), b16),
            pltpu.VMEM((members, tall, LANES), f32),
            pltpu.VMEM((members, tall, LANES), f32),
            pltpu.VMEM((groups, tall, LANES), f32),
            pltpu.VMEM((members, tall, LANES), f32),
            pltpu.VMEM((2 * batch, neig), b16),
            pltpu.VMEM((2 * batch, width), b16),
            pltpu.VMEM((groups, batch, slots), b16),
            dma((1 + groups,)),
            dma((members,)), dma((members,)), dma((groups,)), dma((groups,)),
            dma((members,)), dma((members,)),
            dma((groups * slabs,)), dma((groups * slabs,)),
        ],
        compiler_params=pltpu.CompilerParams(collective_id=1, has_side_effects=True),
    )(field, screening.reshape(1, neig), eigenpotentials, dens)
    return jnp.sum(parts.astype(f32), 0)


def shards(count, slabs, orbitals, eigenpotentials, screening, trial_vectors, pair_index):
    table, trials, pairs = spread(count, slabs, orbitals, trial_vectors, pair_index)
    dens, field = densities(pairs, trials, table)
    slots = trial_vectors.shape[1]
    direct = apply_direct(count, slabs, field, screening, eigenpotentials, dens, slots)
    return jnp.where(pair_index[:1] >= 0, direct, 0.0)


def solution(mesh):
    return jax.shard_map(
        functools.partial(shards, mesh.shape["orb"], mesh.shape["slab"]),
        mesh=mesh,
        in_specs=(P("orb", "slab"), P(None, "slab"), P(), P(None, "orb"), P(None, "orb")),
        out_specs=P(None, "orb"),
        check_vma=False,
    )
```

```python
import functools

import jax
import jax.numpy as jnp
from jax import lax
from jax.experimental import pallas as pl
from jax.experimental.pallas import tpu as pltpu
from jax.sharding import PartitionSpec as P

QUAD = 4
LANES = 128
MESH_ID = pl.DeviceIdType.MESH
VMEM_SPEC = pl.BlockSpec(memory_space=pltpu.VMEM)
ANY_SPEC = pl.BlockSpec(memory_space=pl.ANY)


def greet(peers):
    barrier = pltpu.get_barrier_semaphore()
    for peer in peers:
        pl.semaphore_signal(barrier, inc=1, device_id=peer, device_id_type=MESH_ID)
    return lambda: pl.semaphore_wait(barrier, len(peers))


def flip(index, mask, extent):
    total, bit = 0, 1
    while bit < extent:
        digit = lax.rem(index // bit, 2)
        total = total + bit * (1 - digit if mask & bit else digit)
        bit *= 2
    return total


def columns(start, size):
    return pl.ds(pl.multiple_of(start * size, size), size)


def spread_kernel(
    groups, slabs, orb_hbm, trial_ref, pair_ref, table_ref, trials_ref, pairs_ref, orb_ref,
    own_sem, a_send, a_recv, y_send, y_recv, c_send, c_recv, t_send, t_recv, p_send, p_recv,
    r_send, r_recv,
):
    me, slab = lax.axis_index("orb"), lax.axis_index("slab")
    stage = pltpu.make_async_copy(orb_hbm, orb_ref, own_sem.at[3])
    stage.start()
    group, place = me // QUAD, lax.rem(me, QUAD)
    core = place + 1 - 2 * lax.rem(place, 2)
    side = lax.rem(place + 2, QUAD)
    width = table_ref.shape[2]

    def device(g, q):
        return {"orb": g * QUAD + q}

    others = [lax.rem(group + k, groups) for k in range(1, groups)]
    sources = [lax.rem(group + groups - k, groups) for k in range(1, groups)]
    layers = [lax.rem(slab + k, slabs) for k in range(1, slabs)]
    layer_from = [lax.rem(slab + slabs - k, slabs) for k in range(1, slabs)]
    ready = greet(
        [device(g, place) for g in others]
        + [device(group, core), device(group, side)]
        + [{"slab": x} for x in layers]
    )

    def out_block(g):
        return orb_ref.at[:, columns(g, width)]

    own = pltpu.make_async_copy(out_block(group), table_ref.at[me], own_sem.at[0])
    own_t = pltpu.make_async_copy(trial_ref, trials_ref.at[group], own_sem.at[1])
    own_p = pltpu.make_async_copy(pair_ref, pairs_ref.at[group], own_sem.at[2])
    own_t.start()
    own_p.start()

    def remote(src, dst, send, recv, target):
        return pltpu.make_async_remote_copy(
            src_ref=src, dst_ref=dst, send_sem=send, recv_sem=recv,
            device_id=target, device_id_type=MESH_ID,
        )

    def across(k, sender):
        g = others[k]
        return remote(
            out_block(g), table_ref.at[sender * QUAD + place],
            a_send.at[k], a_recv.at[sender], device(g, place),
        )

    def to_side(k, g, src, q):
        return remote(
            src, table_ref.at[g * QUAD + q], y_send.at[k], y_recv.at[k], device(group, side)
        )

    def to_core(k, g, src, q):
        return remote(
            src, table_ref.at[g * QUAD + q], c_send.at[k], c_recv.at[k], device(group, core)
        )

    def trial_copy(k, sender):
        return remote(
            trial_ref.at[slab], trials_ref.at[sender, slab], t_send.at[k], t_recv.at[sender],
            device(others[k], place),
        )

    def trial_relay(k, n, owner):
        part = trials_ref.at[sources[k], owner]
        slot = k * slabs + n
        return remote(part, part, r_send.at[slot], r_recv.at[slot], {"slab": layers[n]})

    def pair_copy(k, sender):
        return remote(
            pair_ref, pairs_ref.at[sender], p_send.at[k], p_recv.at[sender],
            device(others[k], place),
        )

    stage.wait()
    ready()
    sent = []

    def go(copy):
        copy.start()
        sent.append(copy)

    for k in range(groups - 1):
        go(across(k, group))
    go(to_side(0, group, out_block(group), place))
    go(to_core(0, group, out_block(group), place))
    for k in range(groups - 1):
        go(pair_copy(k, group))
        go(trial_copy(k, group))

    own.start()

    def relay(k):
        g = group if k == 0 else sources[k - 1]
        to_side(k, g, out_block(group), side).wait_recv()
        go(to_core(groups + k, g, table_ref.at[g * QUAD + side], side))

    for k in range(1, groups):
        g = sources[k - 1]
        across(k - 1, g).wait_recv()
        src = table_ref.at[g * QUAD + place]
        go(to_side(k, g, src, place))
        go(to_core(k, g, src, place))
        relay(k - 1)
    for k in range(groups - 1):
        trial_copy(k, sources[k]).wait_recv()
        for n in range(slabs - 1):
            go(trial_relay(k, n, slab))
    relay(groups - 1)
    far = lax.rem(core + 2, QUAD)
    for k in range(groups):
        g = group if k == 0 else sources[k - 1]
        to_core(k, g, out_block(group), core).wait_recv()
        to_core(groups + k, g, out_block(group), far).wait_recv()
    for k in range(groups - 1):
        pair_copy(k, sources[k]).wait_recv()
        for n in range(slabs - 1):
            trial_relay(k, n, layer_from[n]).wait_recv()
    for copy in sent:
        copy.wait_send()
    for copy in (own, own_t, own_p):
        copy.wait()


def spread(count, slabs, orbitals, trial_vectors, pair_index):
    groups = count // QUAD
    batch, slots = trial_vectors.shape
    parts = trial_vectors.reshape(slabs, batch // slabs, slots)
    rows, grid_points = orbitals.shape
    width = grid_points // groups
    dma = pltpu.SemaphoreType.DMA
    table, trials, pairs = pl.pallas_call(
        functools.partial(spread_kernel, groups, slabs),
        out_shape=(
            jax.ShapeDtypeStruct((count, rows, width), orbitals.dtype),
            jax.ShapeDtypeStruct((groups, *parts.shape), parts.dtype),
            jax.ShapeDtypeStruct((groups, *pair_index.shape), pair_index.dtype),
        ),
        in_specs=[ANY_SPEC] * 3,
        out_specs=(ANY_SPEC,) * 3,
        scratch_shapes=[
            pltpu.VMEM((rows, grid_points), orbitals.dtype),
            dma((4,)), dma((groups,)), dma((groups,)), dma((groups,)), dma((groups,)),
            dma((2 * groups,)), dma((2 * groups,)),
            dma((groups,)), dma((groups,)), dma((groups,)), dma((groups,)),
            dma((groups * slabs,)), dma((groups * slabs,)),
        ],
        compiler_params=pltpu.CompilerParams(collective_id=0, has_side_effects=True),
    )(orbitals, parts, pair_index)
    return table, trials.reshape(groups, batch, slots), pairs


def density_kernel(pair_ref, trial_ref, table_ref, dens_ref, field_ref, blocks, sems):
    count, block, width = blocks.shape
    steps = trial_ref.shape[2] // block
    orbs = table_ref.shape[0]
    field_ref[...] = jnp.zeros_like(field_ref)

    def block_index(b):
        return pair_ref[b // steps, :, columns(lax.rem(b, steps), block)]

    def write_out(b):
        return pltpu.make_async_copy(blocks.at[b], dens_ref.at[columns(b, block)], sems.at[b])

    @pl.loop(0, count)
    def _(b):
        index = block_index(b)

        @pl.when(jnp.max(index) >= 0)
        def _():
            ids = lax.broadcasted_iota(jnp.int32, (block, orbs), 1)
            upright = jnp.concatenate([index] * 4, 0).T

            def pick(row):
                hits = ids == upright[:, row : row + 1]
                return jnp.where(hits, 1.0, 0.0).astype(jnp.bfloat16)

            left, right = pick(0), pick(1)
            trial = trial_ref[b // steps, :, columns(lax.rem(b, steps), block)]
            step = min(512, width)
            for c in range(width // step):
                cols = pl.ds(c * step, step)
                part = table_ref[:, cols]
                one = jnp.dot(left, part, preferred_element_type=jnp.float32)
                two = jnp.dot(right, part, preferred_element_type=jnp.float32)
                dens = (one * two).astype(jnp.bfloat16)
                blocks[b, :, cols] = dens
                field_ref[:, cols] += jnp.dot(trial, dens, preferred_element_type=jnp.float32)
            write_out(b).start()

    @pl.loop(0, count)
    def _(b):
        @pl.when(jnp.max(block_index(b)) >= 0)
        def _():
            write_out(b).wait()


def densities(pairs, trials, table):
    groups, batch, slots = trials.shape
    count, rows, width = table.shape
    orbs = count * rows
    block = min(512, slots)
    blocks = groups * slots // block
    return pl.pallas_call(
        density_kernel,
        out_shape=(
            jax.ShapeDtypeStruct((groups * slots, width), jnp.bfloat16),
            jax.ShapeDtypeStruct((batch, width), jnp.float32),
        ),
        in_specs=[VMEM_SPEC] * 3,
        out_specs=(ANY_SPEC, VMEM_SPEC),
        scratch_shapes=[
            pltpu.VMEM((blocks, block, width), jnp.bfloat16),
            pltpu.SemaphoreType.DMA((blocks,)),
        ],
    )(pairs, trials, table.reshape(orbs, width))


def split_rows(values):
    upper = values.astype(jnp.bfloat16)
    lower = (values - upper.astype(jnp.float32)).astype(jnp.bfloat16)
    return jnp.concatenate([upper, lower], 0)


def fold(stacked):
    half = stacked.shape[0] // 2
    return stacked[:half] + stacked[half:]


def apply_kernel(
    count, slabs, field_ref, scale_ref, eig_ref, dens_ref, out_ref,
    eig, dens, pieces, rs_in, outer_in, gathered, screened, potential, shares,
    load_sem, rs_send, rs_recv, z_send, z_recv, ag_send, ag_recv, d_send, d_recv,
):
    me, slab = lax.axis_index("orb"), lax.axis_index("slab")
    groups = count // QUAD
    group, place = me // QUAD, lax.rem(me, QUAD)
    batch, width = field_ref.shape
    slots = out_ref.shape[2]
    members = QUAD * slabs
    tall = pieces.shape[1]
    bands = batch // tall
    mine = place * slabs + slab
    ranks = [lax.rem(mine + k, members) for k in range(1, members)]
    origins = [lax.rem(mine + members - k, members) for k in range(1, members)]
    layers = [lax.rem(slab + k, slabs) for k in range(1, slabs)]
    layer_from = [lax.rem(slab + slabs - k, slabs) for k in range(1, slabs)]
    outers = [flip(group, k, groups) for k in range(groups - 1, 0, -1)]
    goals = outers + [group]

    def member(rank):
        return {"orb": group * QUAD + rank // slabs, "slab": lax.rem(rank, slabs)}

    def keeper(g, x):
        return {"orb": g * QUAD + place, "slab": x}

    peers = [member(r) for r in ranks]
    peers += [keeper(g, x) for g in outers for x in layers + [slab]]
    ready = greet(peers)

    load = pltpu.make_async_copy(eig_ref.at[:, columns(group, width)], eig, load_sem.at[0])
    load.start()
    dens_loads = [
        pltpu.make_async_copy(
            dens_ref.at[pl.ds(g * slots, slots)], dens.at[g], load_sem.at[1 + g]
        )
        for g in range(groups)
    ]
    for copy in dens_loads:
        copy.start()

    def remote(src, dst, send, recv, target):
        return pltpu.make_async_remote_copy(
            src_ref=src, dst_ref=dst, send_sem=send, recv_sem=recv,
            device_id=target, device_id_type=MESH_ID,
        )

    sent = []

    def go(copy):
        copy.start()
        sent.append(copy)

    field = split_rows(field_ref[...])
    load.wait()
    for c in range(eig.shape[0] // LANES):
        part = fold(
            lax.dot_general(
                field, eig[pl.ds(c * LANES, LANES), :], (((1,), (1,)), ((), ())),
                preferred_element_type=jnp.float32,
            )
        )
        for h in range(bands):
            pieces[c * bands + h] = part[h * tall : (h + 1) * tall]

    def scatter(k, sender):
        return remote(
            pieces.at[ranks[k]], rs_in.at[sender], rs_send.at[k], rs_recv.at[sender],
            member(ranks[k]),
        )

    def outer_copy(k, sender):
        return remote(
            outer_in.at[sender], outer_in.at[sender], z_send.at[k], z_recv.at[k],
            keeper(outers[k], slab),
        )

    def gather(k, sender):
        return remote(
            gathered.at[sender], gathered.at[sender], ag_send.at[k], ag_recv.at[sender],
            member(ranks[k]),
        )

    ready()
    for k in range(members - 1):
        go(scatter(k, mine))
    total = pieces[mine]
    for k in range(members - 1):
        scatter(k, origins[k]).wait_recv()
        total = total + rs_in[origins[k]]
    outer_in[group] = total
    for k in range(groups - 1):
        go(outer_copy(k, group))
    for k in range(groups - 1):
        outer_copy(k, outers[k]).wait_recv()
    total = outer_in[0]
    for g in range(1, groups):
        total = total + outer_in[g]
    gathered[mine] = total
    for k in range(members - 1):
        go(gather(k, mine))
    for k in range(members - 1):
        gather(k, origins[k]).wait_recv()
    for c in range(members // bands):
        rows = jnp.concatenate([gathered[c * bands + h] for h in range(bands)], 0)
        cols = slice(c * LANES, (c + 1) * LANES)
        screened[:, cols] = split_rows(rows * scale_ref[:, cols])

    for c in range(width // 256):
        cols = pl.ds(c * 256, 256)
        potential[:, cols] = split_rows(
            fold(jnp.dot(screened[...], eig[:, cols], preferred_element_type=jnp.float32))
        )

    for copy in dens_loads:
        copy.wait()

    def apply_to(g):
        @pl.loop(0, slots // 256)
        def _(c):
            cols = columns(c, 256)
            shares[g, :, cols] = fold(
                lax.dot_general(
                    potential[...], dens[g, cols, :], (((1,), (1,)), ((), ())),
                    preferred_element_type=jnp.float32,
                )
            ).astype(shares.dtype)

    def share_copy(k, n, g, x):
        slot = k * slabs + n
        return remote(
            shares.at[goals[k]], out_ref.at[g * slabs + x], d_send.at[slot], d_recv.at[slot],
            keeper(goals[k], layers[n] if n < slabs - 1 else slab),
        )

    for k in range(groups):
        apply_to(goals[k])
        for n in range(slabs if k < groups - 1 else slabs - 1):
            go(share_copy(k, n, group, slab))
    own = pltpu.make_async_copy(
        shares.at[group], out_ref.at[group * slabs + slab], load_sem.at[0]
    )
    own.start()
    for k in range(groups):
        for n in range(slabs if k < groups - 1 else slabs - 1):
            share_copy(k, n, goals[k], layer_from[n] if n < slabs - 1 else slab).wait_recv()
    own.wait()
    for copy in sent:
        copy.wait_send()


def apply_direct(count, slabs, field, screening, eigenpotentials, dens, slots):
    groups = count // QUAD
    batch, width = field.shape
    neig = eigenpotentials.shape[0]
    members = QUAD * slabs
    tall = batch * neig // (members * LANES)
    dma = pltpu.SemaphoreType.DMA
    f32, b16 = jnp.float32, jnp.bfloat16
    parts = pl.pallas_call(
        functools.partial(apply_kernel, count, slabs),
        out_shape=jax.ShapeDtypeStruct((groups * slabs, batch, slots), b16),
        in_specs=[VMEM_SPEC, VMEM_SPEC, ANY_SPEC, ANY_SPEC],
        out_specs=ANY_SPEC,
        scratch_shapes=[
            pltpu.VMEM((neig, width), b16),
            pltpu.VMEM((groups, slots, width), b16),
            pltpu.VMEM((members, tall, LANES), f32),
            pltpu.VMEM((members, tall, LANES), f32),
            pltpu.VMEM((groups, tall, LANES), f32),
            pltpu.VMEM((members, tall, LANES), f32),
            pltpu.VMEM((2 * batch, neig), b16),
            pltpu.VMEM((2 * batch, width), b16),
            pltpu.VMEM((groups, batch, slots), b16),
            dma((1 + groups,)),
            dma((members,)), dma((members,)), dma((groups,)), dma((groups,)),
            dma((members,)), dma((members,)),
            dma((groups * slabs,)), dma((groups * slabs,)),
        ],
        compiler_params=pltpu.CompilerParams(collective_id=1, has_side_effects=True),
    )(field, screening.reshape(1, neig), eigenpotentials, dens)
    return parts


def shards(count, slabs, orbitals, eigenpotentials, screening, trial_vectors, pair_index):
    table, trials, pairs = spread(count, slabs, orbitals, trial_vectors, pair_index)
    dens, field = densities(pairs, trials, table)
    slots = trial_vectors.shape[1]
    parts = apply_direct(count, slabs, field, screening, eigenpotentials, dens, slots)
    is_live = pair_index[:1][None] >= 0
    return jnp.sum(jnp.where(is_live, parts.astype(jnp.float32), 0.0), 0)


def solution(mesh):
    return jax.shard_map(
        functools.partial(shards, mesh.shape["orb"], mesh.shape["slab"]),
        mesh=mesh,
        in_specs=(P("orb", "slab"), P(None, "slab"), P(), P(None, "orb"), P(None, "orb")),
        out_specs=P(None, "orb"),
        check_vma=False,
    )
```

```python
import functools

import jax
import jax.numpy as jnp
from jax import lax
from jax.experimental import pallas as pl
from jax.experimental.pallas import tpu as pltpu
from jax.sharding import PartitionSpec as P

QUAD = 4
LANES = 128
MESH_ID = pl.DeviceIdType.MESH
VMEM_SPEC = pl.BlockSpec(memory_space=pltpu.VMEM)
ANY_SPEC = pl.BlockSpec(memory_space=pl.ANY)


def greet(peers):
    barrier = pltpu.get_barrier_semaphore()
    for peer in peers:
        pl.semaphore_signal(barrier, inc=1, device_id=peer, device_id_type=MESH_ID)
    return lambda: pl.semaphore_wait(barrier, len(peers))


def flip(index, mask, extent):
    total, bit = 0, 1
    while bit < extent:
        digit = lax.rem(index // bit, 2)
        total = total + bit * (1 - digit if mask & bit else digit)
        bit *= 2
    return total


def columns(start, size):
    return pl.ds(pl.multiple_of(start * size, size), size)


def spread_kernel(
    groups, slabs, orb_hbm, trial_ref, pair_ref, table_ref, trials_ref, pairs_ref, orb_ref,
    own_sem, a_send, a_recv, y_send, y_recv, c_send, c_recv, t_send, t_recv, p_send, p_recv,
    r_send, r_recv,
):
    me, slab = lax.axis_index("orb"), lax.axis_index("slab")
    stage = pltpu.make_async_copy(orb_hbm, orb_ref, own_sem.at[3])
    stage.start()
    group, place = me // QUAD, lax.rem(me, QUAD)
    core = place + 1 - 2 * lax.rem(place, 2)
    side = lax.rem(place + 2, QUAD)
    width = table_ref.shape[2]

    def device(g, q):
        return {"orb": g * QUAD + q}

    others = [lax.rem(group + k, groups) for k in range(1, groups)]
    sources = [lax.rem(group + groups - k, groups) for k in range(1, groups)]
    layers = [lax.rem(slab + k, slabs) for k in range(1, slabs)]
    layer_from = [lax.rem(slab + slabs - k, slabs) for k in range(1, slabs)]
    ready = greet(
        [device(g, place) for g in others]
        + [device(group, core), device(group, side)]
        + [{"slab": x} for x in layers]
    )

    def out_block(g):
        return orb_ref.at[:, columns(g, width)]

    own = pltpu.make_async_copy(out_block(group), table_ref.at[me], own_sem.at[0])
    own_t = pltpu.make_async_copy(trial_ref, trials_ref.at[group], own_sem.at[1])
    own_p = pltpu.make_async_copy(pair_ref, pairs_ref.at[group], own_sem.at[2])
    own_t.start()
    own_p.start()

    def remote(src, dst, send, recv, target):
        return pltpu.make_async_remote_copy(
            src_ref=src, dst_ref=dst, send_sem=send, recv_sem=recv,
            device_id=target, device_id_type=MESH_ID,
        )

    def across(k, sender):
        g = others[k]
        return remote(
            out_block(g), table_ref.at[sender * QUAD + place],
            a_send.at[k], a_recv.at[sender], device(g, place),
        )

    def to_side(k, g, src, q):
        return remote(
            src, table_ref.at[g * QUAD + q], y_send.at[k], y_recv.at[k], device(group, side)
        )

    def to_core(k, g, src, q):
        return remote(
            src, table_ref.at[g * QUAD + q], c_send.at[k], c_recv.at[k], device(group, core)
        )

    def trial_copy(k, sender):
        return remote(
            trial_ref.at[slab], trials_ref.at[sender, slab], t_send.at[k], t_recv.at[sender],
            device(others[k], place),
        )

    def trial_relay(k, n, owner):
        part = trials_ref.at[sources[k], owner]
        slot = k * slabs + n
        return remote(part, part, r_send.at[slot], r_recv.at[slot], {"slab": layers[n]})

    def pair_copy(k, sender):
        return remote(
            pair_ref, pairs_ref.at[sender], p_send.at[k], p_recv.at[sender],
            device(others[k], place),
        )

    stage.wait()
    ready()
    sent = []

    def go(copy):
        copy.start()
        sent.append(copy)

    for k in range(groups - 1):
        go(across(k, group))
    go(to_side(0, group, out_block(group), place))
    go(to_core(0, group, out_block(group), place))
    for k in range(groups - 1):
        go(pair_copy(k, group))
        go(trial_copy(k, group))

    own.start()

    def relay(k):
        g = group if k == 0 else sources[k - 1]
        to_side(k, g, out_block(group), side).wait_recv()
        go(to_core(groups + k, g, table_ref.at[g * QUAD + side], side))

    for k in range(1, groups):
        g = sources[k - 1]
        across(k - 1, g).wait_recv()
        src = table_ref.at[g * QUAD + place]
        go(to_side(k, g, src, place))
        go(to_core(k, g, src, place))
        relay(k - 1)
    for k in range(groups - 1):
        trial_copy(k, sources[k]).wait_recv()
        for n in range(slabs - 1):
            go(trial_relay(k, n, slab))
    relay(groups - 1)
    far = lax.rem(core + 2, QUAD)
    for k in range(groups):
        g = group if k == 0 else sources[k - 1]
        to_core(k, g, out_block(group), core).wait_recv()
        to_core(groups + k, g, out_block(group), far).wait_recv()
    for k in range(groups - 1):
        pair_copy(k, sources[k]).wait_recv()
        for n in range(slabs - 1):
            trial_relay(k, n, layer_from[n]).wait_recv()
    for copy in sent:
        copy.wait_send()
    for copy in (own, own_t, own_p):
        copy.wait()


def spread(count, slabs, orbitals, trial_vectors, pair_index):
    groups = count // QUAD
    batch, slots = trial_vectors.shape
    parts = trial_vectors.reshape(slabs, batch // slabs, slots)
    rows, grid_points = orbitals.shape
    width = grid_points // groups
    dma = pltpu.SemaphoreType.DMA
    table, trials, pairs = pl.pallas_call(
        functools.partial(spread_kernel, groups, slabs),
        out_shape=(
            jax.ShapeDtypeStruct((count, rows, width), orbitals.dtype),
            jax.ShapeDtypeStruct((groups, *parts.shape), parts.dtype),
            jax.ShapeDtypeStruct((groups, *pair_index.shape), pair_index.dtype),
        ),
        in_specs=[ANY_SPEC] * 3,
        out_specs=(ANY_SPEC,) * 3,
        scratch_shapes=[
            pltpu.VMEM((rows, grid_points), orbitals.dtype),
            dma((4,)), dma((groups,)), dma((groups,)), dma((groups,)), dma((groups,)),
            dma((2 * groups,)), dma((2 * groups,)),
            dma((groups,)), dma((groups,)), dma((groups,)), dma((groups,)),
            dma((groups * slabs,)), dma((groups * slabs,)),
        ],
        compiler_params=pltpu.CompilerParams(collective_id=0, has_side_effects=True),
    )(orbitals, parts, pair_index)
    return table, trials.reshape(groups, batch, slots), pairs


def density_kernel(pair_ref, trial_ref, table_ref, dens_ref, field_ref, turned, blocks, sems):
    count, width, block = blocks.shape
    steps = trial_ref.shape[2] // block
    orbs = turned.shape[1]
    turned[...] = table_ref[...].T
    field_ref[...] = jnp.zeros_like(field_ref)

    def block_index(b):
        return pair_ref[b // steps, :, columns(lax.rem(b, steps), block)]

    step = min(512, width)
    chunks = width // step

    def write_out(b, c):
        rows = pl.ds(c * step, step)
        return pltpu.make_async_copy(
            blocks.at[b, rows], dens_ref.at[rows, columns(b, block)], sems.at[b * chunks + c]
        )

    @pl.loop(0, count)
    def _(b):
        index = block_index(b)

        @pl.when(jnp.max(index) >= 0)
        def _():
            ids = lax.broadcasted_iota(jnp.int32, (orbs, block), 0)

            def pick(row):
                return jnp.where(ids == index[row : row + 1], 1.0, 0.0).astype(jnp.bfloat16)

            left, right = pick(0), pick(1)
            trial = trial_ref[b // steps, :, columns(lax.rem(b, steps), block)]
            for c in range(chunks):
                rows = pl.ds(c * step, step)
                part = turned[rows, :]
                one = jnp.dot(part, left, preferred_element_type=jnp.float32)
                two = jnp.dot(part, right, preferred_element_type=jnp.float32)
                dens = (one * two).astype(jnp.bfloat16)
                blocks[b, rows, :] = dens
                write_out(b, c).start()
                field_ref[:, rows] += lax.dot_general(
                    trial, dens, (((1,), (1,)), ((), ())), preferred_element_type=jnp.float32
                )

    @pl.loop(0, count)
    def _(b):
        @pl.when(jnp.max(block_index(b)) >= 0)
        def _():
            for c in range(chunks):
                write_out(b, c).wait()


def densities(pairs, trials, table):
    groups, batch, slots = trials.shape
    count, rows, width = table.shape
    orbs = count * rows
    block = min(512, slots)
    blocks = groups * slots // block
    return pl.pallas_call(
        density_kernel,
        out_shape=(
            jax.ShapeDtypeStruct((width, groups * slots), jnp.bfloat16),
            jax.ShapeDtypeStruct((batch, width), jnp.float32),
        ),
        in_specs=[VMEM_SPEC] * 3,
        out_specs=(ANY_SPEC, VMEM_SPEC),
        scratch_shapes=[
            pltpu.VMEM((width, orbs), jnp.bfloat16),
            pltpu.VMEM((blocks, width, block), jnp.bfloat16),
            pltpu.SemaphoreType.DMA((blocks * (width // min(512, width)),)),
        ],
    )(pairs, trials, table.reshape(orbs, width))


def split_rows(values):
    upper = values.astype(jnp.bfloat16)
    lower = (values - upper.astype(jnp.float32)).astype(jnp.bfloat16)
    return jnp.concatenate([upper, lower], 0)


def fold(stacked):
    half = stacked.shape[0] // 2
    return stacked[:half] + stacked[half:]


def apply_kernel(
    count, slabs, field_ref, scale_ref, eig_ref, dens_ref, out_ref,
    eig, dens, pieces, rs_in, outer_in, gathered, screened, potential, shares,
    load_sem, rs_send, rs_recv, z_send, z_recv, ag_send, ag_recv, d_send, d_recv,
):
    me, slab = lax.axis_index("orb"), lax.axis_index("slab")
    groups = count // QUAD
    group, place = me // QUAD, lax.rem(me, QUAD)
    batch, width = field_ref.shape
    slots = out_ref.shape[2]
    members = QUAD * slabs
    tall = pieces.shape[1]
    bands = batch // tall
    mine = place * slabs + slab
    ranks = [lax.rem(mine + k, members) for k in range(1, members)]
    origins = [lax.rem(mine + members - k, members) for k in range(1, members)]
    layers = [lax.rem(slab + k, slabs) for k in range(1, slabs)]
    layer_from = [lax.rem(slab + slabs - k, slabs) for k in range(1, slabs)]
    outers = [flip(group, k, groups) for k in range(groups - 1, 0, -1)]
    goals = outers + [group]

    def member(rank):
        return {"orb": group * QUAD + rank // slabs, "slab": lax.rem(rank, slabs)}

    def keeper(g, x):
        return {"orb": g * QUAD + place, "slab": x}

    peers = [member(r) for r in ranks]
    peers += [keeper(g, x) for g in outers for x in layers + [slab]]
    ready = greet(peers)

    load = pltpu.make_async_copy(eig_ref.at[:, columns(group, width)], eig, load_sem.at[0])
    load.start()
    dens_loads = [
        pltpu.make_async_copy(
            dens_ref.at[:, pl.ds(g * slots, slots)], dens.at[g], load_sem.at[1 + g]
        )
        for g in range(groups)
    ]
    def remote(src, dst, send, recv, target):
        return pltpu.make_async_remote_copy(
            src_ref=src, dst_ref=dst, send_sem=send, recv_sem=recv,
            device_id=target, device_id_type=MESH_ID,
        )

    sent = []

    def go(copy):
        copy.start()
        sent.append(copy)

    field = split_rows(field_ref[...])
    load.wait()
    for copy in dens_loads:
        copy.start()
    for c in range(eig.shape[0] // LANES):
        part = fold(
            lax.dot_general(
                field, eig[pl.ds(c * LANES, LANES), :], (((1,), (1,)), ((), ())),
                preferred_element_type=jnp.float32,
            )
        )
        for h in range(bands):
            pieces[c * bands + h] = part[h * tall : (h + 1) * tall]

    def scatter(k, sender):
        return remote(
            pieces.at[ranks[k]], rs_in.at[sender], rs_send.at[k], rs_recv.at[sender],
            member(ranks[k]),
        )

    def outer_copy(k, sender):
        return remote(
            outer_in.at[sender], outer_in.at[sender], z_send.at[k], z_recv.at[k],
            keeper(outers[k], slab),
        )

    def gather(k, sender):
        return remote(
            gathered.at[sender], gathered.at[sender], ag_send.at[k], ag_recv.at[sender],
            member(ranks[k]),
        )

    ready()
    for k in range(members - 1):
        go(scatter(k, mine))
    total = pieces[mine]
    for k in range(members - 1):
        scatter(k, origins[k]).wait_recv()
        total = total + rs_in[origins[k]]
    outer_in[group] = total
    for k in range(groups - 1):
        go(outer_copy(k, group))
    for k in range(groups - 1):
        outer_copy(k, outers[k]).wait_recv()
    total = outer_in[0]
    for g in range(1, groups):
        total = total + outer_in[g]
    gathered[mine] = total
    for k in range(members - 1):
        go(gather(k, mine))
    for k in range(members - 1):
        gather(k, origins[k]).wait_recv()
    for c in range(members // bands):
        rows = jnp.concatenate([gathered[c * bands + h] for h in range(bands)], 0)
        cols = slice(c * LANES, (c + 1) * LANES)
        screened[:, cols] = split_rows(rows * scale_ref[:, cols])

    for c in range(width // 256):
        cols = pl.ds(c * 256, 256)
        potential[:, cols] = split_rows(
            fold(jnp.dot(screened[...], eig[:, cols], preferred_element_type=jnp.float32))
        )

    for copy in dens_loads:
        copy.wait()

    def apply_to(g):
        @pl.loop(0, slots // 256)
        def _(c):
            cols = columns(c, 256)
            shares[g, :, cols] = fold(
                jnp.dot(potential[...], dens[g, :, cols], preferred_element_type=jnp.float32)
            ).astype(shares.dtype)

    def share_copy(k, n, g, x):
        slot = k * slabs + n
        return remote(
            shares.at[goals[k]], out_ref.at[g * slabs + x], d_send.at[slot], d_recv.at[slot],
            keeper(goals[k], layers[n] if n < slabs - 1 else slab),
        )

    for k in range(groups):
        apply_to(goals[k])
        for n in range(slabs if k < groups - 1 else slabs - 1):
            go(share_copy(k, n, group, slab))
    own = pltpu.make_async_copy(
        shares.at[group], out_ref.at[group * slabs + slab], load_sem.at[0]
    )
    own.start()
    for k in range(groups):
        for n in range(slabs if k < groups - 1 else slabs - 1):
            share_copy(k, n, goals[k], layer_from[n] if n < slabs - 1 else slab).wait_recv()
    own.wait()
    for copy in sent:
        copy.wait_send()


def apply_direct(count, slabs, field, screening, eigenpotentials, dens, slots):
    groups = count // QUAD
    batch, width = field.shape
    neig = eigenpotentials.shape[0]
    members = QUAD * slabs
    tall = batch * neig // (members * LANES)
    dma = pltpu.SemaphoreType.DMA
    f32, b16 = jnp.float32, jnp.bfloat16
    parts = pl.pallas_call(
        functools.partial(apply_kernel, count, slabs),
        out_shape=jax.ShapeDtypeStruct((groups * slabs, batch, slots), b16),
        in_specs=[VMEM_SPEC, VMEM_SPEC, ANY_SPEC, ANY_SPEC],
        out_specs=ANY_SPEC,
        scratch_shapes=[
            pltpu.VMEM((neig, width), b16),
            pltpu.VMEM((groups, width, slots), b16),
            pltpu.VMEM((members, tall, LANES), f32),
            pltpu.VMEM((members, tall, LANES), f32),
            pltpu.VMEM((groups, tall, LANES), f32),
            pltpu.VMEM((members, tall, LANES), f32),
            pltpu.VMEM((2 * batch, neig), b16),
            pltpu.VMEM((2 * batch, width), b16),
            pltpu.VMEM((groups, batch, slots), b16),
            dma((1 + groups,)),
            dma((members,)), dma((members,)), dma((groups,)), dma((groups,)),
            dma((members,)), dma((members,)),
            dma((groups * slabs,)), dma((groups * slabs,)),
        ],
        compiler_params=pltpu.CompilerParams(collective_id=1, has_side_effects=True),
    )(field, screening.reshape(1, neig), eigenpotentials, dens)
    return parts


def shards(count, slabs, orbitals, eigenpotentials, screening, trial_vectors, pair_index):
    table, trials, pairs = spread(count, slabs, orbitals, trial_vectors, pair_index)
    dens, field = densities(pairs, trials, table)
    slots = trial_vectors.shape[1]
    parts = apply_direct(count, slabs, field, screening, eigenpotentials, dens, slots)
    is_live = pair_index[:1][None] >= 0
    return jnp.sum(jnp.where(is_live, parts.astype(jnp.float32), 0.0), 0)


def solution(mesh):
    return jax.shard_map(
        functools.partial(shards, mesh.shape["orb"], mesh.shape["slab"]),
        mesh=mesh,
        in_specs=(P("orb", "slab"), P(None, "slab"), P(), P(None, "orb"), P(None, "orb")),
        out_specs=P(None, "orb"),
        check_vma=False,
    )
```

```python
import functools

import jax
import jax.numpy as jnp
from jax import lax
from jax.experimental import pallas as pl
from jax.experimental.pallas import tpu as pltpu
from jax.sharding import PartitionSpec as P

QUAD = 4
LANES = 128
MESH_ID = pl.DeviceIdType.MESH
VMEM_SPEC = pl.BlockSpec(memory_space=pltpu.VMEM)
ANY_SPEC = pl.BlockSpec(memory_space=pl.ANY)


def greet(peers):
    barrier = pltpu.get_barrier_semaphore()
    for peer in peers:
        pl.semaphore_signal(barrier, inc=1, device_id=peer, device_id_type=MESH_ID)
    return lambda: pl.semaphore_wait(barrier, len(peers))


def flip(index, mask, extent):
    total, bit = 0, 1
    while bit < extent:
        digit = lax.rem(index // bit, 2)
        total = total + bit * (1 - digit if mask & bit else digit)
        bit *= 2
    return total


def columns(start, size):
    return pl.ds(pl.multiple_of(start * size, size), size)


def spread_kernel(
    groups, slabs, orb_hbm, trial_ref, pair_ref, table_ref, trials_ref, pairs_ref, orb_ref,
    own_sem, a_send, a_recv, y_send, y_recv, c_send, c_recv, t_send, t_recv, p_send, p_recv,
    r_send, r_recv,
):
    me, slab = lax.axis_index("orb"), lax.axis_index("slab")
    stage = pltpu.make_async_copy(orb_hbm, orb_ref, own_sem.at[3])
    stage.start()
    group, place = me // QUAD, lax.rem(me, QUAD)
    core = place + 1 - 2 * lax.rem(place, 2)
    side = lax.rem(place + 2, QUAD)
    width = table_ref.shape[2]

    def device(g, q):
        return {"orb": g * QUAD + q}

    others = [lax.rem(group + k, groups) for k in range(1, groups)]
    sources = [lax.rem(group + groups - k, groups) for k in range(1, groups)]
    layers = [lax.rem(slab + k, slabs) for k in range(1, slabs)]
    layer_from = [lax.rem(slab + slabs - k, slabs) for k in range(1, slabs)]
    ready = greet(
        [device(g, place) for g in others]
        + [device(group, core), device(group, side)]
        + [{"slab": x} for x in layers]
    )

    def out_block(g):
        return orb_ref.at[:, columns(g, width)]

    own = pltpu.make_async_copy(out_block(group), table_ref.at[me], own_sem.at[0])
    own_t = pltpu.make_async_copy(trial_ref, trials_ref.at[group], own_sem.at[1])
    own_p = pltpu.make_async_copy(pair_ref, pairs_ref.at[group], own_sem.at[2])
    own_t.start()
    own_p.start()

    def remote(src, dst, send, recv, target):
        return pltpu.make_async_remote_copy(
            src_ref=src, dst_ref=dst, send_sem=send, recv_sem=recv,
            device_id=target, device_id_type=MESH_ID,
        )

    def across(k, sender):
        g = others[k]
        return remote(
            out_block(g), table_ref.at[sender * QUAD + place],
            a_send.at[k], a_recv.at[sender], device(g, place),
        )

    def to_side(k, g, src, q):
        return remote(
            src, table_ref.at[g * QUAD + q], y_send.at[k], y_recv.at[k], device(group, side)
        )

    def to_core(k, g, src, q):
        return remote(
            src, table_ref.at[g * QUAD + q], c_send.at[k], c_recv.at[k], device(group, core)
        )

    def trial_copy(k, sender):
        return remote(
            trial_ref.at[slab], trials_ref.at[sender, slab], t_send.at[k], t_recv.at[sender],
            device(others[k], place),
        )

    def trial_relay(k, n, owner):
        part = trials_ref.at[sources[k], owner]
        slot = k * slabs + n
        return remote(part, part, r_send.at[slot], r_recv.at[slot], {"slab": layers[n]})

    def pair_copy(k, sender):
        return remote(
            pair_ref, pairs_ref.at[sender], p_send.at[k], p_recv.at[sender],
            device(others[k], place),
        )

    stage.wait()
    ready()
    sent = []

    def go(copy):
        copy.start()
        sent.append(copy)

    for k in range(groups - 1):
        go(across(k, group))
    go(to_side(0, group, out_block(group), place))
    go(to_core(0, group, out_block(group), place))
    for k in range(groups - 1):
        go(pair_copy(k, group))
        go(trial_copy(k, group))

    own.start()

    def relay(k):
        g = group if k == 0 else sources[k - 1]
        to_side(k, g, out_block(group), side).wait_recv()
        go(to_core(groups + k, g, table_ref.at[g * QUAD + side], side))

    for k in range(1, groups):
        g = sources[k - 1]
        across(k - 1, g).wait_recv()
        src = table_ref.at[g * QUAD + place]
        go(to_side(k, g, src, place))
        go(to_core(k, g, src, place))
        relay(k - 1)
    for k in range(groups - 1):
        trial_copy(k, sources[k]).wait_recv()
        for n in range(slabs - 1):
            go(trial_relay(k, n, slab))
    relay(groups - 1)
    far = lax.rem(core + 2, QUAD)
    for k in range(groups):
        g = group if k == 0 else sources[k - 1]
        to_core(k, g, out_block(group), core).wait_recv()
        to_core(groups + k, g, out_block(group), far).wait_recv()
    for k in range(groups - 1):
        pair_copy(k, sources[k]).wait_recv()
        for n in range(slabs - 1):
            trial_relay(k, n, layer_from[n]).wait_recv()
    for copy in sent:
        copy.wait_send()
    for copy in (own, own_t, own_p):
        copy.wait()


def spread(count, slabs, orbitals, trial_vectors, pair_index):
    groups = count // QUAD
    batch, slots = trial_vectors.shape
    parts = trial_vectors.reshape(slabs, batch // slabs, slots)
    rows, grid_points = orbitals.shape
    width = grid_points // groups
    dma = pltpu.SemaphoreType.DMA
    table, trials, pairs = pl.pallas_call(
        functools.partial(spread_kernel, groups, slabs),
        out_shape=(
            jax.ShapeDtypeStruct((count, rows, width), orbitals.dtype),
            jax.ShapeDtypeStruct((groups, *parts.shape), parts.dtype),
            jax.ShapeDtypeStruct((groups, *pair_index.shape), pair_index.dtype),
        ),
        in_specs=[ANY_SPEC] * 3,
        out_specs=(ANY_SPEC,) * 3,
        scratch_shapes=[
            pltpu.VMEM((rows, grid_points), orbitals.dtype),
            dma((4,)), dma((groups,)), dma((groups,)), dma((groups,)), dma((groups,)),
            dma((2 * groups,)), dma((2 * groups,)),
            dma((groups,)), dma((groups,)), dma((groups,)), dma((groups,)),
            dma((groups * slabs,)), dma((groups * slabs,)),
        ],
        compiler_params=pltpu.CompilerParams(collective_id=0, has_side_effects=True),
    )(orbitals, parts, pair_index)
    return table, trials.reshape(groups, batch, slots), pairs


def density_kernel(pair_ref, trial_ref, table_ref, dens_ref, field_ref, turned, blocks, sems):
    count, width, block = blocks.shape
    steps = trial_ref.shape[2] // block
    orbs = turned.shape[1]
    turned[...] = table_ref[...].T
    field_ref[...] = jnp.zeros_like(field_ref)

    def block_index(b):
        return pair_ref[b // steps, :, columns(lax.rem(b, steps), block)]

    def write_out(b):
        return pltpu.make_async_copy(blocks.at[b], dens_ref.at[:, columns(b, block)], sems.at[b])

    @pl.loop(0, count)
    def _(b):
        index = block_index(b)

        @pl.when(jnp.max(index) >= 0)
        def _():
            ids = lax.broadcasted_iota(jnp.int32, (orbs, block), 0)

            def pick(row):
                return jnp.where(ids == index[row : row + 1], 1.0, 0.0).astype(jnp.bfloat16)

            left, right = pick(0), pick(1)
            trial = trial_ref[b // steps, :, columns(lax.rem(b, steps), block)]
            step = min(512, width)
            for c in range(width // step):
                rows = pl.ds(c * step, step)
                part = turned[rows, :]
                one = jnp.dot(part, left, preferred_element_type=jnp.float32)
                two = jnp.dot(part, right, preferred_element_type=jnp.float32)
                dens = (one * two).astype(jnp.bfloat16)
                blocks[b, rows, :] = dens
                field_ref[:, rows] += lax.dot_general(
                    trial, dens, (((1,), (1,)), ((), ())), preferred_element_type=jnp.float32
                )
            write_out(b).start()

    @pl.loop(0, count)
    def _(b):
        @pl.when(jnp.max(block_index(b)) >= 0)
        def _():
            write_out(b).wait()


def densities(pairs, trials, table):
    groups, batch, slots = trials.shape
    count, rows, width = table.shape
    orbs = count * rows
    block = min(512, slots)
    blocks = groups * slots // block
    return pl.pallas_call(
        density_kernel,
        out_shape=(
            jax.ShapeDtypeStruct((width, groups * slots), jnp.bfloat16),
            jax.ShapeDtypeStruct((batch, width), jnp.float32),
        ),
        in_specs=[VMEM_SPEC] * 3,
        out_specs=(ANY_SPEC, VMEM_SPEC),
        scratch_shapes=[
            pltpu.VMEM((width, orbs), jnp.bfloat16),
            pltpu.VMEM((blocks, width, block), jnp.bfloat16),
            pltpu.SemaphoreType.DMA((blocks,)),
        ],
    )(pairs, trials, table.reshape(orbs, width))


def split_rows(values):
    upper = values.astype(jnp.bfloat16)
    lower = (values - upper.astype(jnp.float32)).astype(jnp.bfloat16)
    return jnp.concatenate([upper, lower], 0)


def fold(stacked):
    half = stacked.shape[0] // 2
    return stacked[:half] + stacked[half:]


def apply_kernel(
    count, slabs, field_ref, scale_ref, eig_ref, dens_ref, out_ref,
    eig, dens, pieces, rs_in, outer_in, gathered, screened, potential, shares,
    load_sem, rs_send, rs_recv, z_send, z_recv, ag_send, ag_recv, d_send, d_recv,
):
    me, slab = lax.axis_index("orb"), lax.axis_index("slab")
    groups = count // QUAD
    group, place = me // QUAD, lax.rem(me, QUAD)
    batch, width = field_ref.shape
    slots = out_ref.shape[2]
    members = QUAD * slabs
    tall = pieces.shape[1]
    bands = batch // tall
    mine = place * slabs + slab
    ranks = [lax.rem(mine + k, members) for k in range(1, members)]
    origins = [lax.rem(mine + members - k, members) for k in range(1, members)]
    layers = [lax.rem(slab + k, slabs) for k in range(1, slabs)]
    layer_from = [lax.rem(slab + slabs - k, slabs) for k in range(1, slabs)]
    outers = [flip(group, k, groups) for k in range(groups - 1, 0, -1)]
    goals = outers + [group]

    def member(rank):
        return {"orb": group * QUAD + rank // slabs, "slab": lax.rem(rank, slabs)}

    def keeper(g, x):
        return {"orb": g * QUAD + place, "slab": x}

    peers = [member(r) for r in ranks]
    peers += [keeper(g, x) for g in outers for x in layers + [slab]]
    ready = greet(peers)

    load = pltpu.make_async_copy(eig_ref.at[:, columns(group, width)], eig, load_sem.at[0])
    load.start()
    dens_loads = [
        pltpu.make_async_copy(
            dens_ref.at[:, pl.ds(g * slots, slots)], dens.at[g], load_sem.at[1 + g]
        )
        for g in range(groups)
    ]
    for copy in dens_loads:
        copy.start()

    def remote(src, dst, send, recv, target):
        return pltpu.make_async_remote_copy(
            src_ref=src, dst_ref=dst, send_sem=send, recv_sem=recv,
            device_id=target, device_id_type=MESH_ID,
        )

    sent = []

    def go(copy):
        copy.start()
        sent.append(copy)

    field = split_rows(field_ref[...])
    load.wait()
    for c in range(eig.shape[0] // LANES):
        part = fold(
            lax.dot_general(
                field, eig[pl.ds(c * LANES, LANES), :], (((1,), (1,)), ((), ())),
                preferred_element_type=jnp.float32,
            )
        )
        for h in range(bands):
            pieces[c * bands + h] = part[h * tall : (h + 1) * tall]

    def scatter(k, sender):
        return remote(
            pieces.at[ranks[k]], rs_in.at[sender], rs_send.at[k], rs_recv.at[sender],
            member(ranks[k]),
        )

    def outer_copy(k, sender):
        return remote(
            outer_in.at[sender], outer_in.at[sender], z_send.at[k], z_recv.at[k],
            keeper(outers[k], slab),
        )

    def gather(k, sender):
        return remote(
            gathered.at[sender], gathered.at[sender], ag_send.at[k], ag_recv.at[sender],
            member(ranks[k]),
        )

    ready()
    for k in range(members - 1):
        go(scatter(k, mine))
    total = pieces[mine]
    for k in range(members - 1):
        scatter(k, origins[k]).wait_recv()
        total = total + rs_in[origins[k]]
    outer_in[group] = total
    for k in range(groups - 1):
        go(outer_copy(k, group))
    for k in range(groups - 1):
        outer_copy(k, outers[k]).wait_recv()
    total = outer_in[0]
    for g in range(1, groups):
        total = total + outer_in[g]
    gathered[mine] = total
    for k in range(members - 1):
        go(gather(k, mine))
    for k in range(members - 1):
        gather(k, origins[k]).wait_recv()
    for c in range(members // bands):
        rows = jnp.concatenate([gathered[c * bands + h] for h in range(bands)], 0)
        cols = slice(c * LANES, (c + 1) * LANES)
        screened[:, cols] = split_rows(rows * scale_ref[:, cols])

    for c in range(width // 256):
        cols = pl.ds(c * 256, 256)
        potential[:, cols] = split_rows(
            fold(jnp.dot(screened[...], eig[:, cols], preferred_element_type=jnp.float32))
        )

    for copy in dens_loads:
        copy.wait()

    def apply_to(g):
        @pl.loop(0, slots // 512)
        def _(c):
            cols = columns(c, 512)
            shares[g, :, cols] = fold(
                jnp.dot(potential[...], dens[g, :, cols], preferred_element_type=jnp.float32)
            ).astype(shares.dtype)

    def share_copy(k, n, g, x):
        slot = k * slabs + n
        return remote(
            shares.at[goals[k]], out_ref.at[g * slabs + x], d_send.at[slot], d_recv.at[slot],
            keeper(goals[k], layers[n] if n < slabs - 1 else slab),
        )

    for k in range(groups):
        apply_to(goals[k])
        for n in range(slabs if k < groups - 1 else slabs - 1):
            go(share_copy(k, n, group, slab))
    own = pltpu.make_async_copy(
        shares.at[group], out_ref.at[group * slabs + slab], load_sem.at[0]
    )
    own.start()
    for k in range(groups):
        for n in range(slabs if k < groups - 1 else slabs - 1):
            share_copy(k, n, goals[k], layer_from[n] if n < slabs - 1 else slab).wait_recv()
    own.wait()
    for copy in sent:
        copy.wait_send()


def apply_direct(count, slabs, field, screening, eigenpotentials, dens, slots):
    groups = count // QUAD
    batch, width = field.shape
    neig = eigenpotentials.shape[0]
    members = QUAD * slabs
    tall = batch * neig // (members * LANES)
    dma = pltpu.SemaphoreType.DMA
    f32, b16 = jnp.float32, jnp.bfloat16
    parts = pl.pallas_call(
        functools.partial(apply_kernel, count, slabs),
        out_shape=jax.ShapeDtypeStruct((groups * slabs, batch, slots), b16),
        in_specs=[VMEM_SPEC, VMEM_SPEC, ANY_SPEC, ANY_SPEC],
        out_specs=ANY_SPEC,
        scratch_shapes=[
            pltpu.VMEM((neig, width), b16),
            pltpu.VMEM((groups, width, slots), b16),
            pltpu.VMEM((members, tall, LANES), f32),
            pltpu.VMEM((members, tall, LANES), f32),
            pltpu.VMEM((groups, tall, LANES), f32),
            pltpu.VMEM((members, tall, LANES), f32),
            pltpu.VMEM((2 * batch, neig), b16),
            pltpu.VMEM((2 * batch, width), b16),
            pltpu.VMEM((groups, batch, slots), b16),
            dma((1 + groups,)),
            dma((members,)), dma((members,)), dma((groups,)), dma((groups,)),
            dma((members,)), dma((members,)),
            dma((groups * slabs,)), dma((groups * slabs,)),
        ],
        compiler_params=pltpu.CompilerParams(collective_id=1, has_side_effects=True),
    )(field, screening.reshape(1, neig), eigenpotentials, dens)
    return jnp.sum(parts.astype(f32), 0)


def shards(count, slabs, orbitals, eigenpotentials, screening, trial_vectors, pair_index):
    table, trials, pairs = spread(count, slabs, orbitals, trial_vectors, pair_index)
    dens, field = densities(pairs, trials, table)
    slots = trial_vectors.shape[1]
    direct = apply_direct(count, slabs, field, screening, eigenpotentials, dens, slots)
    return jnp.where(pair_index[:1] >= 0, direct, 0.0)


def solution(mesh):
    return jax.shard_map(
        functools.partial(shards, mesh.shape["orb"], mesh.shape["slab"]),
        mesh=mesh,
        in_specs=(P("orb", "slab"), P(None, "slab"), P(), P(None, "orb"), P(None, "orb")),
        out_specs=P(None, "orb"),
        check_vma=False,
    )
```
